256 devices in a mesh: pairs: 32 (over z, y), aux: 8 (over x, core).
Axes of the slice: x: 4, y: 4, z: 8, core: 2. Of those that a mesh axis runs over, the one named last changes fastest.
Arguments:
- cholesky_slab: bfloat16 [8192, 35840], P('pairs', 'aux'), may hold values from -40 to 40, as said below
- test_matrix: bfloat16 [35840, 768], P('aux', 'pairs'), may hold values from -0.03125 to 0.03125
Outputs:
- projected: float32 [768, 35840], P('pairs', 'aux')
The draws below stay inside these ranges and needn't reach their ends.
Inputs may be any that keep to these rules, and one draw needn't show every extreme that they name: cholesky_slab: real entries with varying row and column magnitudes.
All inputs are finite; a program needn't handle non-finite values.
Results may differ from the reference program's by a relative error of at most 0.0003.
Values may be sent and summed in bfloat16 or wider, within the bound.
A program may use at most 64 MiB of HBM per device.

```python
import math
import jax
import jax.numpy as jnp
from jax import lax

NAUX = 35840
RANK = 768
PAIRS = 8192


def draw_cholesky_slab(key, part):
    keys = jax.random.split(key, 5)
    row_scale = jnp.exp(jax.random.uniform(keys[0], (PAIRS, 1), jnp.float32, math.log(0.3), math.log(3.0)))
    col_scale = jnp.exp(jax.random.uniform(keys[1], (1, NAUX), jnp.float32, math.log(0.3), math.log(3.0)))
    base = jnp.clip(jax.random.normal(keys[4], (PAIRS, NAUX), jnp.float32), -4.0, 4.0)
    return (base * row_scale * col_scale).astype(jnp.bfloat16)


def level_of(stream_key, shape, pieces, low, largest):
    level = 1.0
    for dim, blocks in pieces:
        heights = jax.random.uniform(jax.random.fold_in(jax.random.fold_in(stream_key, 6), dim), (blocks,), jnp.float32, low / len(pieces), largest / len(pieces))
        level = level * jnp.repeat(jnp.exp(heights), shape[dim] // blocks).reshape((-1,) + (1,) * (len(shape) - 1 - dim))
    return level


def gaussian(own_key, shape, deviation, limit, pieces=(), kind=jnp.bfloat16):
    gain = level_of(own_key, shape, pieces, -0.22, 0.18) if pieces else 1.0
    array = jax.random.normal(own_key, shape, jnp.float32) * deviation * gain
    return jnp.minimum(jnp.maximum(array, -limit), limit).astype(kind)


def setup_inputs(seed: int = 0) -> dict:
    seeds = jax.random.split(jax.random.key(seed), 3)
    return {
        "cholesky_slab": draw_cholesky_slab(jax.random.fold_in(seeds[2], 71), 0),
        "test_matrix": gaussian(seeds[1], (NAUX, RANK), NAUX ** -0.5, 0.03125, ((0, 8), (1, 32))),
    }


def reference(cholesky_slab, test_matrix):
    sketch = jnp.dot(cholesky_slab.astype(jnp.float32), test_matrix.astype(jnp.float32), preferred_element_type=jnp.float32)
    gram_matrix = jnp.dot(sketch.T.astype(jnp.float32), sketch.astype(jnp.float32), precision=lax.Precision.HIGHEST, preferred_element_type=jnp.float32)
    lower_factor = jnp.linalg.cholesky(gram_matrix)
    basis_t = jax.scipy.linalg.solve_triangular(lower_factor, sketch.T, lower=True)
    projected = jnp.dot(basis_t.astype(jnp.float32), cholesky_slab.astype(basis_t.dtype).astype(jnp.float32), precision=lax.Precision.HIGHEST, preferred_element_type=jnp.float32)
    return projected
```

```python
import functools
import jax, jax.numpy as jnp
from jax import lax
from jax.experimental import pallas as pl
from jax.experimental.pallas import tpu as pltpu
from jax.sharding import Mesh
from jax.sharding import PartitionSpec as P
HI = lax.Precision.HIGHEST
F32 = jnp.float32
B = 128

def dot(x, y, dims, precision=HI):
    return lax.dot_general(x, y, (dims, ((), ())), precision=precision, preferred_element_type=F32)
NN = ((1,), (0,)); NT = ((1,), (1,)); TN = ((0,), (0,))

def lanes(x, j): return jnp.broadcast_to(x[:, j:j + 1], (x.shape[0], 128))
def row(x, j): return jnp.broadcast_to(x[j:j + 1, :], (8, 128))

def factor_panels(m, v, lo, hi):
    sub = lax.broadcasted_iota(jnp.int32, (8, 128), 0)
    for t in range(lo, hi):
        k = 8 * t
        left, right = m[k:k + 8, :128], m[k:k + 8, 128:]
        cols = [lanes(left, k + j) for j in range(8)]
        d = {(i, j): row(cols[j], i) for i in range(8) for j in range(i + 1)}
        l, inv = {}, []
        for j in range(8):
            r = lax.rsqrt(d[j, j])
            inv.append(r)
            for i in range(j + 1, 8):
                l[i, j] = d[i, j] * r
            for i in range(j + 1, 8):
                for h in range(j + 1, i + 1):
                    d[i, h] = d[i, h] - l[i, j] * l[h, j]
        rows = []
        for part in (left, right):
            raw = [row(part, i) for i in range(8)]
            done = []
            for i in range(8):
                x = raw[i]
                for j in range(i):
                    x = x - l[i, j] * done[j]
                done.append(x * inv[i])
            rows.append(done)
        tile = rows[1][0]
        for i in range(1, 8):
            tile = jnp.where(sub == i, rows[1][i], tile)
        v[k:k + 8, :] = tile
        if t < 15:
            q = []
            for done in rows:
                back = [None] * 8
                for i in reversed(range(8)):
                    x = done[i]
                    for j in range(i + 1, 8):
                        x = x - l[j, i] * back[j]
                    back[i] = x * inv[i]
                q.append(back)
            e = k + 8
            ml, mr = m[e:, :128], m[e:, 128:]
            al, ar = ml, mr
            for i in range(8):
                c = jnp.broadcast_to(ml[:, k + i:k + i + 1], ml.shape)
                al = al - c * q[0][i][:1, :]
                ar = ar - c * q[1][i][:1, :]
            m[e:, :128] = al
            m[e:, 128:] = ar

def chol_block(a, w, lfac, m, v, b, n=6):
    s, e = b * B, (b + 1) * B
    vb = v[...]
    w[s:e, s:e] = vb
    if b:
        part = dot(lfac[s:e, :s], w[:s, :s], NN)
        w[s:e, :s] = -dot(vb, part, NN)
    if b < n - 1:
        lfac[e:, s:e] = dot(a[e:, s:e], vb, NT)
        for j in range(b + 1, n):
            js, je = j * B, (j + 1) * B
            a[js:, js:je] = a[js:, js:je] - dot(lfac[js:, s:e], lfac[js:je, s:e], NT)

MESH = pl.DeviceIdType.MESH
NZ, NY, NX = 8, 4, 4
AXES = ("z", "y", "x", "c")
SIZES = {"z": NZ, "y": NY, "x": NX, "c": 2}
VM = pl.BlockSpec(memory_space=pltpu.VMEM)
ANY = pl.BlockSpec(memory_space=pl.ANY)
DMA = pltpu.SemaphoreType.DMA


def step_to(axis, hops):
    return lax.rem(lax.axis_index(axis) + hops, SIZES[axis])


def greet(peers):
    barrier = pltpu.get_barrier_semaphore()
    for axis, hops in peers:
        pl.semaphore_signal(barrier, inc=1, device_id={axis: step_to(axis, hops)}, device_id_type=MESH)
    pl.semaphore_wait(barrier, len(peers))


def send(src, dst, sems, k, axis, hops):
    copy = pltpu.make_async_remote_copy(
        src_ref=src, dst_ref=dst, send_sem=sems[0].at[k], recv_sem=sems[1].at[k],
        device_id={axis: step_to(axis, hops)}, device_id_type=MESH,
    )
    copy.start()
    return copy


def ring_gather(block, own, axis, cuts, sems, base):
    n = SIZES[axis]
    me = lax.axis_index(axis)
    lo, mid, hi = cuts
    far = n // 2
    copies = []
    for s in range(far):
        last = s == far - 1
        pair = []
        for k, way in enumerate((1, n - 1)):
            if last:
                a, b = (lo, mid) if k == 0 else (mid, hi)
            else:
                a, b = lo, hi
            who = lax.rem(me + (n - s if k == 0 else s), n)
            src = own(a, b) if s == 0 else block(who, a, b)
            pair.append(send(src, block(who, a, b), sems, base + 2 * s + k, axis, way))
        copies += pair
        yield copies
        for c in pair:
            c.wait_recv()


def gather_kernel(t, g, send_sems, recv_sems, own_sem):
    z, y = lax.axis_index("z"), lax.axis_index("y")
    K = t.shape[1]
    sems = (send_sems, recv_sems)
    cut = 14 * 128
    keep = pltpu.make_async_copy(t, g.at[z, y], own_sem)
    keep.start()
    greet([("y", 1), ("y", NY - 1), ("z", 1), ("z", NZ - 1)])
    own = lambda a, b: t.at[:, a:b]
    lcuts, rcuts = (0, 7 * 128, cut), (cut, cut + 11 * 128, K)
    ly = ring_gather(lambda i, a, b: g.at[z, i, :, a:b], own, "y", lcuts, sems, 0)
    rz = ring_gather(lambda i, a, b: g.at[i, y, :, a:b], own, "z", rcuts, sems, 4)
    lz = ring_gather(lambda i, a, b: g.at[i, :, :, a:b], lambda a, b: g.at[z, :, :, a:b], "z", lcuts, sems, 12)
    ry = ring_gather(lambda i, a, b: g.at[:, i, :, a:b], lambda a, b: g.at[:, y, :, a:b], "y", rcuts, sems, 20)
    done = []
    def go(gen, times=1):
        for _ in range(times):
            try:
                held = next(gen)
                if not any(h is held for h in done):
                    done.append(held)
            except StopIteration:
                return
    go(ly); go(rz); go(ly); go(rz); go(ly)
    keep.wait()
    go(lz); go(rz); go(rz); go(rz); go(ry)
    go(lz); go(lz); go(ry); go(lz); go(lz); go(ry)
    for held in done:
        for c in held:
            c.wait_send()


def gather(t):
    d, K = t.shape
    g = pl.pallas_call(
        gather_kernel, out_shape=jax.ShapeDtypeStruct((NZ, NY, d, K), t.dtype),
        in_specs=[ANY], out_specs=ANY,
        scratch_shapes=[DMA((24,)), DMA((24,)), DMA],
        compiler_params=pltpu.CompilerParams(collective_id=0, has_side_effects=True), name="gather",
    )(t)
    return g.reshape(NZ * NY * d, K)


def total_kernel(part, out, near, acc, far, send_sems, recv_sems):
    x, c = lax.axis_index("x"), lax.axis_index("c")
    R = part.shape[0]
    h, q = R // 2, R // 8
    sems = (send_sems, recv_sems)
    greet([("c", 1)] + [("x", i) for i in (1, 2, 3)])
    mine = pl.multiple_of(c * h, h)
    other = pl.multiple_of((1 - c) * h, h)
    first = send(part.at[pl.ds(other, h)], near, sems, 0, "c", 1)
    first.wait_recv()
    acc[...] = part[pl.ds(mine, h), :] + near[...]
    spread = []
    for i in (1, 2, 3):
        o = pl.multiple_of(step_to("x", i) * q, q)
        spread.append(send(acc.at[pl.ds(o, q)], far.at[i - 1], sems, i, "x", i))
    o = pl.multiple_of(x * q, q)
    total = acc[pl.ds(o, q), :]
    for i in (1, 2, 3):
        spread[i - 1].wait_recv()
        total = total + far[i - 1]
    own = pl.ds(pl.multiple_of(mine + o, q), q)
    out[own, :] = total
    back = [send(out.at[own], out.at[own], sems, 3 + i, "x", i) for i in (1, 2, 3)]
    for b in back:
        b.wait_recv()
    half = out.at[pl.ds(mine, h)]
    last = send(half, half, sems, 7, "c", 1)
    last.wait_recv()
    for copy in (first, *spread, *back, last):
        copy.wait_send()


def total_over_aux(part):
    R, C = part.shape
    return pl.pallas_call(
        total_kernel, out_shape=jax.ShapeDtypeStruct((R, C), F32),
        in_specs=[VM], out_specs=VM,
        scratch_shapes=[pltpu.VMEM((R // 2, C), F32), pltpu.VMEM((R // 2, C), F32), pltpu.VMEM((3, R // 8, C), F32), DMA((8,)), DMA((8,))],
        compiler_params=pltpu.CompilerParams(collective_id=1, has_side_effects=True), name="total",
    )(part)


SLOTS = 3


def place(t):
    at_least = lambda k: (t + 32 - k) // 32
    i = at_least(1) + at_least(3) + at_least(6) + at_least(10) + at_least(15)
    j = t - i * (i + 1) // 2
    spare = at_least(21)
    return i, j * (1 - spare)


def gram_compute(s, gp):
    a = lax.axis_index("x") * 2 + lax.axis_index("c")
    for k in range(SLOTS):
        i, j = place(a * SLOTS + k)
        li = s[:, pl.ds(pl.multiple_of(i * B, B), B)]
        lj = s[:, pl.ds(pl.multiple_of(j * B, B), B)]
        gp[k * B:(k + 1) * B, :] = dot(li, lj, TN)


GRAM_PEERS = [("z", i) for i in range(1, NZ)] + [("y", i) for i in range(1, NY)] + [("x", i) for i in range(1, NX)] + [("c", 1)]
GRAM_COPIES = 7 + 3 + 7 + 3 + 1


def gram_exchange(gp, gz, own, gy, full, sems, base):
    x, c, z = lax.axis_index("x"), lax.axis_index("c"), lax.axis_index("z")
    q = gp.shape[0] // NZ
    copies = []
    ones = []
    for i in range(1, NZ):
        o = pl.multiple_of(step_to("z", i) * q, q)
        ones.append(send(gp.at[pl.ds(o, q)], gz.at[i - 1], sems, base + i - 1, "z", i))
    yield
    mine = pl.ds(pl.multiple_of(z * q, q), q)
    total = gp[mine, :]
    for i in range(1, NZ):
        ones[i - 1].wait_recv()
        total = total + gz[i - 1]
    own[...] = total
    twos = [send(own, gy.at[i - 1], sems, base + 6 + i, "y", i) for i in range(1, NY)]
    yield
    total = own[...]
    for i in range(1, NY):
        twos[i - 1].wait_recv()
        total = total + gy[i - 1]
    full[x, c, mine, :] = total
    here = full.at[x, c, mine]
    threes = [send(here, here, sems, base + 9 + i, "z", i) for i in range(1, NZ)]
    yield
    for t in threes:
        t.wait_recv()
    all_mine = full.at[x, c]
    fours = [send(all_mine, all_mine, sems, base + 16 + i, "x", i) for i in range(1, NX)]
    yield
    for t in fours:
        t.wait_recv()
    column = full.at[:, c]
    five = send(column, column, sems, base + 20, "c", 1)
    yield
    five.wait_recv()
    for t in (*ones, *twos, *threes, *fours, five):
        t.wait_send()


GRAM_SCRATCH = [pltpu.VMEM((SLOTS * B, B), F32), pltpu.VMEM((NZ - 1, SLOTS * B // NZ, B), F32), pltpu.VMEM((SLOTS * B // NZ, B), F32), pltpu.VMEM((NY - 1, SLOTS * B // NZ, B), F32)]


HALF = 384


class Stream:
    def __init__(self, axis, way, local, buf, sink, sems, base):
        self.axis, self.way, self.n = axis, way, SIZES[axis]
        self.local, self.buf, self.sink, self.sems, self.base = local, buf, sink, sems, base

    def block(self, back):
        n = self.n
        return lax.rem(lax.axis_index(self.axis) + (2 * n - back if self.way == 1 else back), n)

    def copy(self, s):
        return pltpu.make_async_remote_copy(
            src_ref=self.local(self.block(1)) if s == 0 else self.buf.at[s - 1],
            dst_ref=self.buf.at[s],
            send_sem=self.sems[0].at[self.base + s], recv_sem=self.sems[1].at[self.base + s],
            device_id={self.axis: step_to(self.axis, 1 if self.way == 1 else self.n - 1)}, device_id_type=MESH,
        )

    def serve(self, s):
        self.copy(s).wait_recv()
        total = self.buf[s] + self.local(self.block(2 + s))[...]
        if s < self.n - 2:
            self.buf[s] = total
            self.copy(s + 1).start()
        else:
            self.sink[...] = total

    def finish(self):
        for s in range(self.n - 1):
            self.copy(s).wait_send()


def sub_start(i):
    return pl.multiple_of(i * 140 // 8 * 8, 8)


Z_ROWS = ((1, 0, 144), (1, 144, 136), (-1, 280, 144), (-1, 424, 136))
Y_ROWS = ((1, 0, 40), (1, 40, 32), (-1, 72, 40), (-1, 112, 32))
ZY_ROWS = ((1, 0, 72), (-1, 72, 72))
RS_COPIES = 4 * 7 + 4 * 3 + 2 * 3 + 4 * 7


def finish_kernel(slab, s, out, w, c, resz, resy, *rest):
    zb, yb, zyb, yzb = rest[0:4], rest[4:8], rest[8:10], rest[10:14]
    hi, lo, gp, gz, own, gy, full, a, lfac, m, v, ss, rs, gs, gr = rest[14:]
    sems = (ss, rs)
    tiles = slab.shape[1] // B
    greet(GRAM_PEERS)
    exchange = gram_exchange(gp, gz, own, gy, full, (gs, gr), 0)
    gram_compute(s, gp)
    next(exchange)
    hi[...] = s[...].astype(jnp.bfloat16)
    lo[...] = (s[...] - hi[...].astype(F32)).astype(jnp.bfloat16)

    def tile(t, _):
        part = slab[:, pl.ds(pl.multiple_of(t * B, B), B)]
        value = lax.dot_general(part, hi[...], (TN, ((), ())), preferred_element_type=F32)
        value = value + lax.dot_general(part, lo[...], (TN, ((), ())), preferred_element_type=F32)
        for k in range(8):
            q = t * 8 + k
            c[q // 35, pl.ds(pl.multiple_of(lax.rem(q, 35) * 16, 16), 16), :] = value[k * 16:(k + 1) * 16, :]
        return 0

    lax.fori_loop(0, 20, tile, 0)
    next(exchange)
    lax.fori_loop(20, tiles, tile, 0)
    next(exchange)

    base = 0
    zs, ys, zys, yzs = [], [], [], []
    for k, (way, o, n) in enumerate(Z_ROWS):
        local = lambda i, o=o, n=n: c.at[i, o:o + n, 0:HALF]
        zs.append(Stream("z", way, local, zb[k], resz.at[o:o + n], sems, base))
        base += NZ - 1
    for k, (way, o, n) in enumerate(Y_ROWS):
        local = lambda i, o=o, n=n: c.at[:, pl.ds(sub_start(i) + o, n), HALF:2 * HALF]
        ys.append(Stream("y", way, local, yb[k], resy.at[:, o:o + n], sems, base))
        base += NY - 1
    for k, (way, o, n) in enumerate(ZY_ROWS):
        local = lambda i, o=o, n=n: resz.at[pl.ds(sub_start(i) + o, n)]
        zys.append(Stream("y", way, local, zyb[k], out.at[o:o + n, 0:HALF], sems, base))
        base += NY - 1
    for k, (way, o, n) in enumerate(Y_ROWS):
        local = lambda i, o=o, n=n: resy.at[i, o:o + n]
        yzs.append(Stream("z", way, local, yzb[k], out.at[o:o + n, HALF:2 * HALF], sems, base))
        base += NZ - 1
    for k in (0, 2, 1, 3):
        zs[k].copy(0).start()
        ys[k].copy(0).start()

    events = []
    def later(when, action):
        events.append((when, len(events), action))
    for step in range(NZ - 1):
        for k in (0, 2, 1, 3):
            later(9.3 * (step + 1) + (1.7 if k % 2 else -2.9), lambda k=k, step=step: zs[k].serve(step))
    for step in range(NY - 1):
        for k in (0, 2, 1, 3):
            later(19 * (step + 1) + (1.7 if k % 2 else -6.8), lambda k=k, step=step: ys[k].serve(step))
    later(67, lambda: [x.copy(0).start() for x in zys])
    later(58.8, lambda: [yzs[k].copy(0).start() for k in (0, 2, 1, 3)])
    for step in range(NY - 1):
        for k in (0, 1):
            later(71 + 4 * step, lambda k=k, step=step: zys[k].serve(step))
    for step in range(NZ - 1):
        for k in (0, 2, 1, 3):
            later(62.5 + 3.3 * step, lambda k=k, step=step: yzs[k].serve(step))
    events.sort(key=lambda e: e[:2])

    def due(now):
        ready = []
        while events and events[0][0] <= now:
            ready.append(events.pop(0)[2])
        return ready

    next(exchange)
    now = 8
    for cost in (10, 4):
        for action in due(now):
            action()
        now += cost
        try:
            next(exchange)
        except StopIteration:
            pass
    for action in due(now):
        action()
    for _ in exchange:
        pass
    n = 6
    for i in range(n):
        for j in range(i + 1):
            t = i * (i + 1) // 2 + j
            a[i * B:(i + 1) * B, j * B:(j + 1) * B] = full[t // 6, t // 3 % 2, (t % 3) * B:(t % 3 + 1) * B, :]
    w[...] = jnp.zeros_like(w)
    row_of = lax.broadcasted_iota(jnp.int32, (B, B), 0)
    col_of = lax.broadcasted_iota(jnp.int32, (B, B), 1)
    eye = jnp.where(row_of == col_of, 1.0, 0.0).astype(F32)
    table = {}
    for b in range(n):
        for piece in range(4):
            now += 1.35
            table[b, piece] = due(now)
            now += 0.3 * len(table[b, piece])
        now += 2

    def step(b, _):
        o = pl.multiple_of(b * B, B)
        m[:, :B] = a[pl.ds(o, B), pl.ds(o, B)]
        m[:, B:] = eye
        for piece in range(4):
            factor_panels(m, v, 4 * piece, 4 * piece + 4)
            for k in range(n):
                if table[k, piece]:
                    @pl.when(b == k)
                    def _():
                        for action in table[k, piece]:
                            action()
        for k in range(n):
            @pl.when(b == k)
            def _():
                chol_block(a, w, lfac, m, v, k)
        return 0

    lax.fori_loop(0, n, step, 0)
    for action in due(1e9):
        action()
    for stream in (*zs, *ys, *zys, *yzs):
        stream.finish()


def finish(slab, s):
    bf = jnp.bfloat16
    R, C = s.shape
    vm = lambda *shape: pltpu.VMEM(shape, F32)
    return pl.pallas_call(
        finish_kernel,
        out_shape=(jax.ShapeDtypeStruct((144, C), F32), jax.ShapeDtypeStruct((C, C), F32)),
        in_specs=[VM, VM], out_specs=(VM, VM),
        scratch_shapes=[
            vm(NZ, 560, C), vm(560, HALF), vm(NZ, 144, HALF),
            *[vm(NZ - 1, n, HALF) for _, _, n in Z_ROWS],
            *[vm(NY - 1, NZ, n, HALF) for _, _, n in Y_ROWS],
            *[vm(NY - 1, n, HALF) for _, _, n in ZY_ROWS],
            *[vm(NZ - 1, n, HALF) for _, _, n in Y_ROWS],
            pltpu.VMEM((R, C), bf), pltpu.VMEM((R, C), bf),
            *GRAM_SCRATCH, vm(NX, 2, SLOTS * B, B), vm(C, C), vm(C, C), vm(B, 2 * B), vm(B, B),
            DMA((RS_COPIES,)), DMA((RS_COPIES,)), DMA((GRAM_COPIES,)), DMA((GRAM_COPIES,)),
        ],
        compiler_params=pltpu.CompilerParams(collective_id=2, has_side_effects=True, vmem_limit_bytes=60 * 2**20), name="finish",
    )(slab, s)


def body(slab, test):
    tests = gather(test.T)
    part = lax.dot_general(slab, tests, (NT, ((), ())), preferred_element_type=F32)
    sketch = total_over_aux(part)
    c, w = finish(slab, sketch)
    y = lax.axis_index("y")
    c = lax.dynamic_slice_in_dim(c, y * 140 % 8, 140, 0)
    p = lax.dot_general(w, c, (NT, ((), ())), precision=HI, preferred_element_type=F32)
    p = lax.all_to_all(p.reshape(NZ * NY, 24, -1), ("z", "y"), 0, 0, tiled=True)
    return p.transpose(1, 0, 2).reshape(24, -1)


def solution(mesh):
    split = Mesh(mesh.devices.reshape(NZ, NY, NX, 2), AXES)
    return jax.shard_map(
        body, mesh=split, in_specs=(P(("z", "y"), ("x", "c")), P(("x", "c"), ("z", "y"))),
        out_specs=P(("z", "y"), ("x", "c")), check_vma=False,
    )
```

```python
import functools
import heapq
import jax, jax.numpy as jnp
from jax import lax
from jax.experimental import pallas as pl
from jax.experimental.pallas import tpu as pltpu
from jax.sharding import Mesh
from jax.sharding import PartitionSpec as P
HI = lax.Precision.HIGHEST
F32 = jnp.float32
B = 128

def dot(x, y, dims, precision=HI):
    return lax.dot_general(x, y, (dims, ((), ())), precision=precision, preferred_element_type=F32)
NN = ((1,), (0,)); NT = ((1,), (1,)); TN = ((0,), (0,))

def lanes(x, j): return jnp.broadcast_to(x[:, j:j + 1], (x.shape[0], 128))
def row(x, j): return jnp.broadcast_to(x[j:j + 1, :], (8, 128))

def factor_panels(m, v, lo, hi):
    sub = lax.broadcasted_iota(jnp.int32, (8, 128), 0)
    for t in range(lo, hi):
        k = 8 * t
        left, right = m[k:k + 8, :128], m[k:k + 8, 128:]
        cols = [lanes(left, k + j) for j in range(8)]
        d = {(i, j): row(cols[j], i) for i in range(8) for j in range(i + 1)}
        l, inv = {}, []
        for j in range(8):
            r = lax.rsqrt(d[j, j])
            inv.append(r)
            for i in range(j + 1, 8):
                l[i, j] = d[i, j] * r
            for i in range(j + 1, 8):
                for h in range(j + 1, i + 1):
                    d[i, h] = d[i, h] - l[i, j] * l[h, j]
        rows = []
        for part in (left, right):
            raw = [row(part, i) for i in range(8)]
            done = []
            for i in range(8):
                x = raw[i]
                for j in range(i):
                    x = x - l[i, j] * done[j]
                done.append(x * inv[i])
            rows.append(done)
        tile = rows[1][0]
        for i in range(1, 8):
            tile = jnp.where(sub == i, rows[1][i], tile)
        v[k:k + 8, :] = tile
        if t < 15:
            q = []
            for done in rows:
                back = [None] * 8
                for i in reversed(range(8)):
                    x = done[i]
                    for j in range(i + 1, 8):
                        x = x - l[j, i] * back[j]
                    back[i] = x * inv[i]
                q.append(back)
            e = k + 8
            ml, mr = m[e:, :128], m[e:, 128:]
            al, ar = ml, mr
            for i in range(8):
                c = jnp.broadcast_to(ml[:, k + i:k + i + 1], ml.shape)
                al = al - c * q[0][i][:1, :]
                ar = ar - c * q[1][i][:1, :]
            m[e:, :128] = al
            m[e:, 128:] = ar

def chol_block(a, w, lfac, m, v, b, n=6):
    s, e = b * B, (b + 1) * B
    vb = v[...]
    w[s:e, s:e] = vb
    if b:
        part = dot(lfac[s:e, :s], w[:s, :s], NN)
        w[s:e, :s] = -dot(vb, part, NN)
    if b < n - 1:
        lfac[e:, s:e] = dot(a[e:, s:e], vb, NT)
        for j in range(b + 1, n):
            js, je = j * B, (j + 1) * B
            a[js:, js:je] = a[js:, js:je] - dot(lfac[js:, s:e], lfac[js:je, s:e], NT)

MESH = pl.DeviceIdType.MESH
NZ, NY, NX = 8, 4, 4
AXES = ("z", "y", "x", "c")
SIZES = {"z": NZ, "y": NY, "x": NX, "c": 2}
VM = pl.BlockSpec(memory_space=pltpu.VMEM)
ANY = pl.BlockSpec(memory_space=pl.ANY)
DMA = pltpu.SemaphoreType.DMA


def step_to(axis, hops):
    return lax.rem(lax.axis_index(axis) + hops, SIZES[axis])


def greet(peers):
    barrier = pltpu.get_barrier_semaphore()
    for axis, hops in peers:
        pl.semaphore_signal(barrier, inc=1, device_id={axis: step_to(axis, hops)}, device_id_type=MESH)
    pl.semaphore_wait(barrier, len(peers))


def send(src, dst, sems, k, axis, hops):
    copy = pltpu.make_async_remote_copy(
        src_ref=src, dst_ref=dst, send_sem=sems[0].at[k], recv_sem=sems[1].at[k],
        device_id={axis: step_to(axis, hops)}, device_id_type=MESH,
    )
    copy.start()
    return copy


RATE, HOP = 42e3, 2.0


def gather_plan(d, cut, K):
    free, heap, plan, count = {}, [], [], 0

    def start(now, phase, way, step, dz, dy, lo, hi):
        nonlocal count
        axis = phase[1]
        begin = max(now, free.get((axis, way), 0.0))
        end = begin + d * (hi - lo) * 2 / RATE
        free[axis, way] = end
        job = (phase, axis, way, step, dz, dy, lo, hi, count)
        count += 1
        heapq.heappush(heap, (end + HOP, count, job))
        return job

    def both(now, phase, dz, dy, lo, hi):
        return [start(now, phase, way, 0, dz, dy, lo, hi) for way in (1, -1)]

    first = both(0, "ly", 0, 0, 0, cut) + both(0, "rz", 0, 0, cut, K)
    first += both(0, "lz", 0, 0, 0, cut) + both(0, "ry", 0, 0, cut, K)
    plan.append((None, first))
    now = 0.0
    while heap:
        when, _, job = heapq.heappop(heap)
        now = max(now, when) + 0.05
        phase, axis, way, step, dz, dy, lo, hi, _ = job
        dz, dy = (dz - way, dy) if axis == "z" else (dz, dy - way)
        mid = lo + ((hi - lo) // 128 + 1) // 2 * 128
        far = SIZES[axis] // 2
        new = []
        if step < far - 1:
            a, b = (lo, hi) if step < far - 2 else ((lo, mid) if way == 1 else (mid, hi))
            if b > a:
                new.append(start(now, phase, way, step + 1, dz, dy, a, b))
        if phase in ("ly", "rz"):
            new += both(now, "lz" if phase == "ly" else "ry", dz, dy, lo, hi)
        plan.append((job, new))
    return plan, count, now


def gather_kernel(plan, t, g, send_sems, recv_sems, own_sem):
    z, y = lax.axis_index("z"), lax.axis_index("y")

    def copy(job):
        phase, axis, way, step, dz, dy, lo, hi, k = job
        place = g.at[lax.rem(z + dz + NZ, NZ), lax.rem(y + dy + NY, NY), :, lo:hi]
        return pltpu.make_async_remote_copy(
            src_ref=t.at[:, lo:hi] if dz == dy == 0 else place, dst_ref=place,
            send_sem=send_sems.at[k], recv_sem=recv_sems.at[k],
            device_id={axis: step_to(axis, 1 if way == 1 else SIZES[axis] - 1)}, device_id_type=MESH,
        )

    greet([("y", 1), ("y", NY - 1), ("z", 1), ("z", NZ - 1)])
    for job, new in plan:
        if job is not None:
            copy(job).wait_recv()
        for other in new:
            copy(other).start()
        if job is None:
            keep = pltpu.make_async_copy(t, g.at[z, y], own_sem)
            keep.start()
    keep.wait()
    for job, _ in plan[1:]:
        copy(job).wait_send()


def gather(t):
    d, K = t.shape
    plan, count, _ = gather_plan(d, K // 128 * 2 // 5 * 128, K)
    g = pl.pallas_call(
        functools.partial(gather_kernel, plan), out_shape=jax.ShapeDtypeStruct((NZ, NY, d, K), t.dtype),
        in_specs=[ANY], out_specs=ANY,
        scratch_shapes=[DMA((count,)), DMA((count,)), DMA],
        compiler_params=pltpu.CompilerParams(collective_id=0, has_side_effects=True), name="gather",
    )(t)
    return g.reshape(NZ * NY * d, K)


def total_kernel(part, out, near, acc, far, send_sems, recv_sems):
    x, c = lax.axis_index("x"), lax.axis_index("c")
    R = part.shape[0]
    h, q = R // 2, R // 8
    sems = (send_sems, recv_sems)
    greet([("c", 1)] + [("x", i) for i in (1, 2, 3)])
    mine = pl.multiple_of(c * h, h)
    other = pl.multiple_of((1 - c) * h, h)
    first = send(part.at[pl.ds(other, h)], near, sems, 0, "c", 1)
    first.wait_recv()
    acc[...] = part[pl.ds(mine, h), :] + near[...]
    spread = []
    for i in (1, 2, 3):
        o = pl.multiple_of(step_to("x", i) * q, q)
        spread.append(send(acc.at[pl.ds(o, q)], far.at[i - 1], sems, i, "x", i))
    o = pl.multiple_of(x * q, q)
    total = acc[pl.ds(o, q), :]
    for i in (1, 2, 3):
        spread[i - 1].wait_recv()
        total = total + far[i - 1]
    own = pl.ds(pl.multiple_of(mine + o, q), q)
    out[own, :] = total
    back = [send(out.at[own], out.at[own], sems, 3 + i, "x", i) for i in (1, 2, 3)]
    for b in back:
        b.wait_recv()
    half = out.at[pl.ds(mine, h)]
    last = send(half, half, sems, 7, "c", 1)
    last.wait_recv()
    for copy in (first, *spread, *back, last):
        copy.wait_send()


def total_over_aux(part):
    R, C = part.shape
    return pl.pallas_call(
        total_kernel, out_shape=jax.ShapeDtypeStruct((R, C), F32),
        in_specs=[VM], out_specs=VM,
        scratch_shapes=[pltpu.VMEM((R // 2, C), F32), pltpu.VMEM((R // 2, C), F32), pltpu.VMEM((3, R // 8, C), F32), DMA((8,)), DMA((8,))],
        compiler_params=pltpu.CompilerParams(collective_id=1, has_side_effects=True), name="total",
    )(part)


SLOTS = 3


def place(t):
    at_least = lambda k: (t + 32 - k) // 32
    i = at_least(1) + at_least(3) + at_least(6) + at_least(10) + at_least(15)
    j = t - i * (i + 1) // 2
    spare = at_least(21)
    return i, j * (1 - spare)


def gram_compute(s, gp):
    a = lax.axis_index("x") * 2 + lax.axis_index("c")
    for k in range(SLOTS):
        i, j = place(a * SLOTS + k)
        li = s[:, pl.ds(pl.multiple_of(i * B, B), B)]
        lj = s[:, pl.ds(pl.multiple_of(j * B, B), B)]
        gp[k * B:(k + 1) * B, :] = dot(li, lj, TN)


GRAM_PEERS = [("z", i) for i in range(1, NZ)] + [("y", i) for i in range(1, NY)] + [("x", i) for i in range(1, NX)] + [("c", 1)]
GRAM_COPIES = 7 + 3 + 7 + 3 + 1


def gram_exchange(gp, gz, own, gy, full, sems, base):
    x, c, z = lax.axis_index("x"), lax.axis_index("c"), lax.axis_index("z")
    q = gp.shape[0] // NZ
    copies = []
    ones = []
    for i in range(1, NZ):
        o = pl.multiple_of(step_to("z", i) * q, q)
        ones.append(send(gp.at[pl.ds(o, q)], gz.at[i - 1], sems, base + i - 1, "z", i))
    yield
    mine = pl.ds(pl.multiple_of(z * q, q), q)
    total = gp[mine, :]
    for i in range(1, NZ):
        ones[i - 1].wait_recv()
        total = total + gz[i - 1]
    own[...] = total
    twos = [send(own, gy.at[i - 1], sems, base + 6 + i, "y", i) for i in range(1, NY)]
    yield
    total = own[...]
    for i in range(1, NY):
        twos[i - 1].wait_recv()
        total = total + gy[i - 1]
    full[x, c, mine, :] = total
    here = full.at[x, c, mine]
    threes = [send(here, here, sems, base + 9 + i, "z", i) for i in range(1, NZ)]
    yield
    for t in threes:
        t.wait_recv()
    all_mine = full.at[x, c]
    fours = [send(all_mine, all_mine, sems, base + 16 + i, "x", i) for i in range(1, NX)]
    yield
    for t in fours:
        t.wait_recv()
    column = full.at[:, c]
    five = send(column, column, sems, base + 20, "c", 1)
    yield
    five.wait_recv()
    for t in (*ones, *twos, *threes, *fours, five):
        t.wait_send()


GRAM_SCRATCH = [pltpu.VMEM((SLOTS * B, B), F32), pltpu.VMEM((NZ - 1, SLOTS * B // NZ, B), F32), pltpu.VMEM((SLOTS * B // NZ, B), F32), pltpu.VMEM((NY - 1, SLOTS * B // NZ, B), F32)]


Z_ROWS = ((1, 0, 144), (1, 144, 136), (-1, 280, 144), (-1, 424, 136))
Y_ROWS = ((1, 0, 40), (1, 40, 32), (-1, 72, 40), (-1, 112, 32))
ZY_ROWS = ((1, 0, 72), (-1, 72, 72))
HALF = 384
KINDS = (("z", "z", Z_ROWS), ("y", "y", Y_ROWS), ("zy", "y", ZY_ROWS), ("yz", "z", Y_ROWS))


def stream_specs():
    specs = []
    for kind, axis, rows in KINDS:
        for k, (way, o, n) in enumerate(rows):
            after = {"zy": tuple(("z", i) for i in range(4)), "yz": (("y", k),)}.get(kind, ())
            specs.append(((kind, k), axis, way, n * HALF * 4 * (NZ if kind == "y" else 1), after))
    return specs


def finish_plan():
    specs = {s[0]: s for s in stream_specs()}
    free, heap, plan, count, ended = {}, [], [], 0, set()

    def wire(now, axis, way, size):
        end = max(now, free.get((axis, way), 0.0)) + size / RATE
        free[axis, way] = end
        return end + HOP

    def post(when, what):
        nonlocal count
        count += 1
        heapq.heappush(heap, (when, count, what))

    def begin(now, name):
        _, axis, way, size, _ = specs[name]
        post(wire(now, axis, way, size), ("serve", name, 0))

    def gram_sends(now, stage):
        q = SLOTS * B * B * 4 // NZ
        if stage in (0, 2):
            when = max(wire(now, "z", way, 8 * q) for way in (1, -1)) + 1.5 * HOP
        elif stage == 1:
            when = max(wire(now, "y", way, 2 * q) for way in (1, -1)) + HOP
        else:
            when = now + (11.0 if stage == 3 else 3.5)
        post(when, ("gram", stage + 1))

    now = 1.5
    gram_sends(now, 0)
    now += 3.0
    zfirst = [n for n, s in specs.items() if not s[4] and s[1] == "z"]
    yfirst = [n for n, s in specs.items() if not s[4] and s[1] == "y"]
    early = zfirst[0:3:2]
    held = {1: yfirst, 2: [n for n in zfirst if n not in early]}

    def launch(names):
        for name in names:
            begin(now, name)
        plan.append(("begin", names))

    launch(early)
    plan.append(("tiles",))
    now += 3.4
    chol = []
    while heap or chol:
        if heap and (heap[0][0] <= now or not chol):
            when, _, what = heapq.heappop(heap)
            now = max(now, when)
            plan.append(what)
            if what[0] == "gram":
                now += 0.3
                if what[1] < 5:
                    gram_sends(now, what[1])
                    launch(held.get(what[1], []))
                else:
                    now += 1.0
                    chol = [c for b in range(6) for c in [("chol", b, p) for p in range(4)] + [("block", b)]]
            else:
                _, name, s = what
                _, axis, way, size, _ = specs[name]
                now += 0.1 + size / 3e6
                if s < SIZES[axis] - 2:
                    post(wire(now, axis, way, size), ("serve", name, s + 1))
                else:
                    ended.add(name)
                    for other, spec in specs.items():
                        if name in spec[4] and all(x in ended for x in spec[4]):
                            begin(now, other)
                            plan.append(("begin", [other]))
        else:
            what = chol.pop(0)
            plan.append(what)
            now += 1.35 if what[0] == "chol" else 2.0
            chol_end = now
    return plan, now, chol_end


class Stream:
    def __init__(self, axis, way, local, buf, sink, sems, base):
        self.axis, self.way, self.n = axis, way, SIZES[axis]
        self.local, self.buf, self.sink, self.sems, self.base = local, buf, sink, sems, base

    def block(self, back):
        n = self.n
        return lax.rem(lax.axis_index(self.axis) + (2 * n - back if self.way == 1 else back), n)

    def copy(self, s):
        return pltpu.make_async_remote_copy(
            src_ref=self.local(self.block(1)) if s == 0 else self.buf.at[s - 1],
            dst_ref=self.buf.at[s],
            send_sem=self.sems[0].at[self.base + s], recv_sem=self.sems[1].at[self.base + s],
            device_id={self.axis: step_to(self.axis, 1 if self.way == 1 else self.n - 1)}, device_id_type=MESH,
        )

    def serve(self, s):
        self.copy(s).wait_recv()
        total = self.buf[s] + self.local(self.block(2 + s))[...]
        if s < self.n - 2:
            self.buf[s] = total
            self.copy(s + 1).start()
        else:
            self.sink[...] = total

    def finish(self):
        for s in range(self.n - 1):
            self.copy(s).wait_send()


def sub_start(i):
    return pl.multiple_of(i * 140 // 8 * 8, 8)


RS_COPIES = 4 * 7 + 4 * 3 + 2 * 3 + 4 * 7


def finish_kernel(slab, s, out, w, c, resz, resy, *rest):
    zb, yb, zyb, yzb = rest[0:4], rest[4:8], rest[8:10], rest[10:14]
    hi, lo, gp, gz, own, gy, full, a, lfac, m, v, ss, rs, gs, gr = rest[14:]
    sems = (ss, rs)
    tiles = slab.shape[1] // B
    greet(GRAM_PEERS)
    exchange = gram_exchange(gp, gz, own, gy, full, (gs, gr), 0)
    gram_compute(s, gp)
    next(exchange)
    hi[...] = s[...].astype(jnp.bfloat16)
    lo[...] = (s[...] - hi[...].astype(F32)).astype(jnp.bfloat16)

    def tile(t, _):
        part = slab[:, pl.ds(pl.multiple_of(t * B, B), B)]
        value = lax.dot_general(part, hi[...], (TN, ((), ())), preferred_element_type=F32)
        value = value + lax.dot_general(part, lo[...], (TN, ((), ())), preferred_element_type=F32)
        for k in range(8):
            q = t * 8 + k
            c[q // 35, pl.ds(pl.multiple_of(lax.rem(q, 35) * 16, 16), 16), :] = value[k * 16:(k + 1) * 16, :]
        return 0

    start = lax.rem(lax.axis_index("z") + NZ - 1, NZ) * (slab.shape[1] // NZ) // B
    early = 15

    def tiles_of(lo, hi):
        lax.fori_loop(lo, hi, lambda t, _: tile(lax.rem(start + t, tiles), 0), 0)

    streams, base = {}, 0
    for kind, axis, rows in KINDS:
        for k, (way, o, n) in enumerate(rows):
            buf, sink = {
                "z": lambda: (zb[k], resz.at[o:o + n]),
                "y": lambda: (yb[k], resy.at[:, o:o + n]),
                "zy": lambda: (zyb[k], out.at[o:o + n, 0:HALF]),
                "yz": lambda: (yzb[k], out.at[o:o + n, HALF:2 * HALF]),
            }[kind]()
            local = functools.partial(lambda i, kind, o, n: {
                "z": lambda: c.at[i, o:o + n, 0:HALF],
                "y": lambda: c.at[:, pl.ds(sub_start(i) + o, n), HALF:2 * HALF],
                "zy": lambda: resz.at[pl.ds(sub_start(i) + o, n)],
                "yz": lambda: resy.at[i, o:o + n],
            }[kind](), kind=kind, o=o, n=n)
            streams[kind, k] = Stream(axis, way, local, buf, sink, sems, base)
            base += SIZES[axis] - 1

    n = 6

    def act(what):
        if what[0] == "gram":
            next(exchange, None)
            if what[1] == 5:
                for i in range(n):
                    for j in range(i + 1):
                        t = i * (i + 1) // 2 + j
                        a[i * B:(i + 1) * B, j * B:(j + 1) * B] = full[t // 6, t // 3 % 2, (t % 3) * B:(t % 3 + 1) * B, :]
        elif what[0] == "begin":
            for name in what[1]:
                streams[name].copy(0).start()
        elif what[0] == "serve":
            streams[what[1]].serve(what[2])
        elif what[0] == "tiles":
            tiles_of(early, tiles)

    plan = finish_plan()[0]
    first = next(i for i, what in enumerate(plan) if what[0] == "chol")
    last = max(i for i, what in enumerate(plan) if what[0] == "block")
    table, key = {}, None
    for what in plan[first:last + 1]:
        if what[0] == "chol":
            key = what[1], what[2]
        elif what[0] == "block":
            key = what[1], 4
        else:
            table.setdefault(key, []).append(what)

    tiles_of(0, early)
    w[...] = jnp.zeros_like(w)
    for what in plan[:first]:
        act(what)
    row_of = lax.broadcasted_iota(jnp.int32, (B, B), 0)
    col_of = lax.broadcasted_iota(jnp.int32, (B, B), 1)
    eye = jnp.where(row_of == col_of, 1.0, 0.0).astype(F32)

    def step(b, _):
        o = pl.multiple_of(b * B, B)
        m[:, :B] = a[pl.ds(o, B), pl.ds(o, B)]
        m[:, B:] = eye
        for piece in range(5):
            if piece < 4:
                factor_panels(m, v, 4 * piece, 4 * piece + 4)
            for k in range(n):
                if piece == 4 or table.get((k, piece)):
                    @pl.when(b == k)
                    def _():
                        if piece == 4:
                            chol_block(a, w, lfac, m, v, k)
                        for what in table.get((k, piece), ()):
                            act(what)
        return 0

    lax.fori_loop(0, n, step, 0)
    for what in plan[last + 1:]:
        act(what)
    for stream in streams.values():
        stream.finish()


def finish(slab, s):
    bf = jnp.bfloat16
    R, C = s.shape
    vm = lambda *shape: pltpu.VMEM(shape, F32)
    return pl.pallas_call(
        finish_kernel,
        out_shape=(jax.ShapeDtypeStruct((144, C), F32), jax.ShapeDtypeStruct((C, C), F32)),
        in_specs=[VM, VM], out_specs=(VM, VM),
        scratch_shapes=[
            vm(NZ, 560, C), vm(560, HALF), vm(NZ, 144, HALF),
            *[vm(NZ - 1, n, HALF) for _, _, n in Z_ROWS],
            *[vm(NY - 1, NZ, n, HALF) for _, _, n in Y_ROWS],
            *[vm(NY - 1, n, HALF) for _, _, n in ZY_ROWS],
            *[vm(NZ - 1, n, HALF) for _, _, n in Y_ROWS],
            pltpu.VMEM((R, C), bf), pltpu.VMEM((R, C), bf),
            *GRAM_SCRATCH, vm(NX, 2, SLOTS * B, B), vm(C, C), vm(C, C), vm(B, 2 * B), vm(B, B),
            DMA((RS_COPIES,)), DMA((RS_COPIES,)), DMA((GRAM_COPIES,)), DMA((GRAM_COPIES,)),
        ],
        compiler_params=pltpu.CompilerParams(collective_id=2, has_side_effects=True, vmem_limit_bytes=60 * 2**20), name="finish",
    )(slab, s)


def body(slab, test):
    tests = gather(test.T)
    part = lax.dot_general(slab, tests, (NT, ((), ())), preferred_element_type=F32)
    sketch = total_over_aux(part)
    c, w = finish(slab, sketch)
    y = lax.axis_index("y")
    c = lax.dynamic_slice_in_dim(c, y * 140 % 8, 140, 0)
    p = lax.dot_general(w, c, (NT, ((), ())), precision=HI, preferred_element_type=F32)
    p = lax.all_to_all(p.reshape(NZ * NY, 24, -1), ("z", "y"), 0, 0, tiled=True)
    return p.transpose(1, 0, 2).reshape(24, -1)


def solution(mesh):
    split = Mesh(mesh.devices.reshape(NZ, NY, NX, 2), AXES)
    return jax.shard_map(
        body, mesh=split, in_specs=(P(("z", "y"), ("x", "c")), P(("x", "c"), ("z", "y"))),
        out_specs=P(("z", "y"), ("x", "c")), check_vma=False,
    )
```

```python
import functools
import heapq
import jax, jax.numpy as jnp
from jax import lax
from jax.experimental import pallas as pl
from jax.experimental.pallas import tpu as pltpu
from jax.sharding import Mesh
from jax.sharding import PartitionSpec as P
HI = lax.Precision.HIGHEST
F32 = jnp.float32
B = 128

def dot(x, y, dims, precision=HI):
    return lax.dot_general(x, y, (dims, ((), ())), precision=precision, preferred_element_type=F32)
NN = ((1,), (0,)); NT = ((1,), (1,)); TN = ((0,), (0,))

def lanes(x, j): return jnp.broadcast_to(x[:, j:j + 1], (x.shape[0], 128))
def row(x, j): return jnp.broadcast_to(x[j:j + 1, :], (8, 128))

def factor_panels(m, v, lo, hi):
    sub = lax.broadcasted_iota(jnp.int32, (8, 128), 0)
    for t in range(lo, hi):
        k = 8 * t
        left, right = m[k:k + 8, :128], m[k:k + 8, 128:]
        cols = [lanes(left, k + j) for j in range(8)]
        d = {(i, j): row(cols[j], i) for i in range(8) for j in range(i + 1)}
        l, inv = {}, []
        for j in range(8):
            r = lax.rsqrt(d[j, j])
            inv.append(r)
            for i in range(j + 1, 8):
                l[i, j] = d[i, j] * r
            for i in range(j + 1, 8):
                for h in range(j + 1, i + 1):
                    d[i, h] = d[i, h] - l[i, j] * l[h, j]
        rows = []
        for part in (left, right):
            raw = [row(part, i) for i in range(8)]
            done = []
            for i in range(8):
                x = raw[i]
                for j in range(i):
                    x = x - l[i, j] * done[j]
                done.append(x * inv[i])
            rows.append(done)
        tile = rows[1][0]
        for i in range(1, 8):
            tile = jnp.where(sub == i, rows[1][i], tile)
        v[k:k + 8, :] = tile
        if t < 15:
            q = []
            for done in rows:
                back = [None] * 8
                for i in reversed(range(8)):
                    x = done[i]
                    for j in range(i + 1, 8):
                        x = x - l[j, i] * back[j]
                    back[i] = x * inv[i]
                q.append(back)
            e = k + 8
            ml, mr = m[e:, :128], m[e:, 128:]
            al, ar = ml, mr
            for i in range(8):
                c = jnp.broadcast_to(ml[:, k + i:k + i + 1], ml.shape)
                al = al - c * q[0][i][:1, :]
                ar = ar - c * q[1][i][:1, :]
            m[e:, :128] = al
            m[e:, 128:] = ar

def chol_block(a, w, lfac, m, v, b, n=6):
    s, e = b * B, (b + 1) * B
    vb = v[...]
    w[s:e, s:e] = vb
    if b:
        part = dot(lfac[s:e, :s], w[:s, :s], NN)
        w[s:e, :s] = -dot(vb, part, NN)
    if b < n - 1:
        lfac[e:, s:e] = dot(a[e:, s:e], vb, NT)
        for j in range(b + 1, n):
            js, je = j * B, (j + 1) * B
            a[js:, js:je] = a[js:, js:je] - dot(lfac[js:, s:e], lfac[js:je, s:e], NT)

MESH = pl.DeviceIdType.MESH
NZ, NY, NX = 8, 4, 4
AXES = ("z", "y", "x", "c")
SIZES = {"z": NZ, "y": NY, "x": NX, "c": 2}
VM = pl.BlockSpec(memory_space=pltpu.VMEM)
ANY = pl.BlockSpec(memory_space=pl.ANY)
DMA = pltpu.SemaphoreType.DMA


def step_to(axis, hops):
    return lax.rem(lax.axis_index(axis) + hops, SIZES[axis])


def greet(peers):
    barrier = pltpu.get_barrier_semaphore()
    for axis, hops in peers:
        pl.semaphore_signal(barrier, inc=1, device_id={axis: step_to(axis, hops)}, device_id_type=MESH)
    pl.semaphore_wait(barrier, len(peers))


def send(src, dst, sems, k, axis, hops):
    copy = pltpu.make_async_remote_copy(
        src_ref=src, dst_ref=dst, send_sem=sems[0].at[k], recv_sem=sems[1].at[k],
        device_id={axis: step_to(axis, hops)}, device_id_type=MESH,
    )
    copy.start()
    return copy


RATE, HOP = 42e3, 2.0


def sketch_plan(d, cut, K):
    free, heap, plan, count, order = {}, [], [], 0, 0
    missing = {dz: NY * K for dz in range(NZ)}

    def post(when, what):
        nonlocal order
        order += 1
        heapq.heappush(heap, (when, order, what))

    def start(now, phase, way, step, dz, dy, lo, hi):
        nonlocal count
        axis = phase[1]
        end = max(now, free.get((axis, way), 0.0)) + d * (hi - lo) * 2 / RATE
        free[axis, way] = end
        job = (phase, axis, way, step, dz, dy, lo, hi, count)
        count += 1
        post(end + HOP, ("got", job))
        return job

    def both(now, phase, dz, dy, lo, hi):
        return [start(now, phase, way, 0, dz, dy, lo, hi) for way in (1, -1)]

    def share(now, axis, size, lag):
        end = max(now, free.get(axis, 0.0)) + size / (100e3 if axis == "c" else RATE / 2)
        free[axis] = end
        return end + lag

    first = both(0, "ly", 0, 0, 0, cut) + both(0, "rz", 0, 0, cut, K)
    first += both(0, "lz", 0, 0, 0, cut) + both(0, "ry", 0, 0, cut, K)
    plan.append(("got", None, first))
    missing[0] -= K
    now = 0.0
    rows = NY * d
    while heap:
        when, _, what = heapq.heappop(heap)
        now = max(now, when) + 0.05
        if what[0] == "got":
            job = what[1]
            phase, axis, way, step, dz, dy, lo, hi, _ = job
            dz, dy = (dz - way, dy) if axis == "z" else (dz, dy - way)
            mid = lo + ((hi - lo) // 128 + 1) // 2 * 128
            far = SIZES[axis] // 2
            new = []
            if step < far - 1:
                a, b = (lo, hi) if step < far - 2 else ((lo, mid) if way == 1 else (mid, hi))
                if b > a:
                    new.append(start(now, phase, way, step + 1, dz, dy, a, b))
            if phase in ("ly", "rz"):
                new += both(now, "lz" if phase == "ly" else "ry", dz, dy, lo, hi)
            plan.append(("got", job, new))
            missing[dz % NZ] -= hi - lo
            if not missing[dz % NZ]:
                post(now + 0.3, ("product", dz % NZ))
        elif what[0] == "product":
            plan.append(what)
            now += 1.5
            post(share(now, "c", rows * 512, 1.5), ("sum", what[1], 1))
        else:
            _, dz, stage = what
            plan.append(what)
            now += 0.2
            if stage < 3:
                post(share(now, "x", rows * 128 * 3, HOP + 1), ("sum", dz, stage + 1))
            elif stage == 3:
                post(share(now, "c", rows * 512, 1.5), ("sum", dz, 4))
    return plan, count, now


def sketch_kernel(plan, t, slab, st, g, part, near, acc, far, gs, gr, ss, sr, own_sem):
    z, y, x, c = (lax.axis_index(axis) for axis in AXES)
    d = t.shape[0] * 8
    rows, piece = NY * d, NY * d // NX
    half = st.shape[1] // 2

    def place(dz, dy, lo, hi):
        at = (lax.rem(z + dz + NZ, NZ) * NY + lax.rem(y + dy + NY, NY)) * d
        return g.at[pl.ds(at // 8, d // 8), :, lo:hi]

    def copy(job):
        phase, axis, way, step, dz, dy, lo, hi, k = job
        to = place(dz, dy, lo, hi)
        return pltpu.make_async_remote_copy(
            src_ref=t.at[:, :, lo:hi] if dz == dy == 0 else to, dst_ref=to, send_sem=gs.at[k], recv_sem=gr.at[k],
            device_id={axis: step_to(axis, 1 if way == 1 else SIZES[axis] - 1)}, device_id_type=MESH,
        )

    def rows_of(dz):
        return pl.multiple_of(lax.rem(z + dz, NZ) * rows, 8)

    def lanes_of(core):
        return pl.ds(pl.multiple_of(core * half, half), half)

    def remote(src, dst, k, axis, hops):
        return pltpu.make_async_remote_copy(
            src_ref=src, dst_ref=dst, send_sem=ss.at[k], recv_sem=sr.at[k],
            device_id={axis: step_to(axis, hops)}, device_id_type=MESH,
        )

    def exchange(dz, stage):
        k = dz * 8
        if stage == 1:
            return [remote(part.at[dz, :, lanes_of(1 - c)], near.at[dz], k, "c", 1)]
        if stage == 2:
            return [remote(acc.at[dz, pl.ds(pl.multiple_of(step_to("x", i) * piece, 8), piece)], far.at[dz, i - 1], k + i, "x", i) for i in (1, 2, 3)]
        if stage == 3:
            own = st.at[pl.ds(pl.multiple_of(rows_of(dz) + x * piece, 8), piece), lanes_of(c)]
            return [remote(own, own, k + 3 + i, "x", i) for i in (1, 2, 3)]
        all_mine = st.at[pl.ds(rows_of(dz), rows), lanes_of(c)]
        return [remote(all_mine, all_mine, k + 7, "c", 1)]

    def begin(dz, stage):
        for one in exchange(dz, stage):
            one.start()

    greet([("y", 1), ("y", NY - 1), ("z", 1), ("z", NZ - 1), ("c", 1)] + [("x", i) for i in (1, 2, 3)])
    keep = pltpu.make_async_copy(t, place(0, 0, 0, t.shape[2]), own_sem)
    kept = False
    for what in plan:
        if what[0] == "got":
            if what[1] is not None:
                copy(what[1]).wait_recv()
            for job in what[2]:
                copy(job).start()
            if what[1] is None:
                keep.start()
        elif what[0] == "product":
            dz = what[1]
            if not kept:
                keep.wait()
                kept = True
            part[dz] = lax.dot_general(g[pl.ds(rows_of(dz) // 8, rows // 8)].reshape(rows, g.shape[2]), slab[...], (NT, ((), ())), preferred_element_type=F32)
            begin(dz, 1)
        else:
            _, dz, stage = what
            for one in exchange(dz, stage):
                one.wait_recv()
            if stage == 1:
                acc[dz] = part[dz, :, lanes_of(c)] + near[dz]
            elif stage == 2:
                mine = pl.multiple_of(x * piece, 8)
                total = acc[dz, pl.ds(mine, piece), :]
                for i in range(3):
                    total = total + far[dz, i]
                st[pl.ds(pl.multiple_of(rows_of(dz) + mine, 8), piece), lanes_of(c)] = total
            if stage < 4:
                begin(dz, stage + 1)
    for what in plan:
        if what[0] == "got" and what[1] is not None:
            copy(what[1]).wait_send()
        elif what[0] == "sum":
            for one in exchange(what[1], what[2]):
                one.wait_send()


def sketch_of(t, slab):
    d, K = t.shape
    R = slab.shape[0]
    plan, count, _ = sketch_plan(d, K // 128 * 2 // 5 * 128, K)
    n, rows = NZ * NY * d, NY * d
    return pl.pallas_call(
        functools.partial(sketch_kernel, plan),
        out_shape=jax.ShapeDtypeStruct((n, R), F32),
        in_specs=[ANY, VM], out_specs=VM,
        scratch_shapes=[
            pltpu.VMEM((n // 8, 8, K), t.dtype),
            pltpu.VMEM((NZ, rows, R), F32), pltpu.VMEM((NZ, rows, R // 2), F32), pltpu.VMEM((NZ, rows, R // 2), F32),
            pltpu.VMEM((NZ, 3, rows // NX, R // 2), F32), DMA((count,)), DMA((count,)), DMA((64,)), DMA((64,)), DMA,
        ],
        compiler_params=pltpu.CompilerParams(collective_id=0, has_side_effects=True, vmem_limit_bytes=40 * 2**20), name="sketch",
    )(t.reshape(d // 8, 8, K), slab)


SLOTS = 3


def place(t):
    at_least = lambda k: (t + 32 - k) // 32
    i = at_least(1) + at_least(3) + at_least(6) + at_least(10) + at_least(15)
    j = t - i * (i + 1) // 2
    spare = at_least(21)
    return i, j * (1 - spare)


def gram_compute(s, gp):
    a = lax.axis_index("x") * 2 + lax.axis_index("c")
    for k in range(SLOTS):
        i, j = place(a * SLOTS + k)
        li = s[pl.ds(pl.multiple_of(i * B, B), B), :]
        lj = s[pl.ds(pl.multiple_of(j * B, B), B), :]
        gp[k * B:(k + 1) * B, :] = dot(li, lj, NT)


GRAM_PEERS = [("z", i) for i in range(1, NZ)] + [("y", i) for i in range(1, NY)] + [("x", i) for i in range(1, NX)] + [("c", 1)]
GRAM_COPIES = 7 + 3 + 7 + 3 + 1


def gram_exchange(gp, gz, own, gy, full, sems, base):
    x, c, z = lax.axis_index("x"), lax.axis_index("c"), lax.axis_index("z")
    q = gp.shape[0] // NZ
    copies = []
    ones = []
    for i in range(1, NZ):
        o = pl.multiple_of(step_to("z", i) * q, q)
        ones.append(send(gp.at[pl.ds(o, q)], gz.at[i - 1], sems, base + i - 1, "z", i))
    yield
    mine = pl.ds(pl.multiple_of(z * q, q), q)
    total = gp[mine, :]
    for i in range(1, NZ):
        ones[i - 1].wait_recv()
        total = total + gz[i - 1]
    own[...] = total
    twos = [send(own, gy.at[i - 1], sems, base + 6 + i, "y", i) for i in range(1, NY)]
    yield
    total = own[...]
    for i in range(1, NY):
        twos[i - 1].wait_recv()
        total = total + gy[i - 1]
    full[x, c, mine, :] = total
    here = full.at[x, c, mine]
    threes = [send(here, here, sems, base + 9 + i, "z", i) for i in range(1, NZ)]
    yield
    for t in threes:
        t.wait_recv()
    all_mine = full.at[x, c]
    fours = [send(all_mine, all_mine, sems, base + 16 + i, "x", i) for i in range(1, NX)]
    yield
    for t in fours:
        t.wait_recv()
    column = full.at[:, c]
    five = send(column, column, sems, base + 20, "c", 1)
    yield
    five.wait_recv()
    for t in (*ones, *twos, *threes, *fours, five):
        t.wait_send()


GRAM_SCRATCH = [pltpu.VMEM((SLOTS * B, B), F32), pltpu.VMEM((NZ - 1, SLOTS * B // NZ, B), F32), pltpu.VMEM((SLOTS * B // NZ, B), F32), pltpu.VMEM((NY - 1, SLOTS * B // NZ, B), F32)]


Z_ROWS = ((1, 0, 144), (1, 144, 136), (-1, 280, 144), (-1, 424, 136))
Y_ROWS = ((1, 0, 40), (1, 40, 32), (-1, 72, 40), (-1, 112, 32))
ZY_ROWS = ((1, 0, 72), (-1, 72, 72))
HALF = 384
KINDS = (("z", "z", Z_ROWS), ("y", "y", Y_ROWS), ("zy", "y", ZY_ROWS), ("yz", "z", Y_ROWS))


def stream_specs():
    specs = []
    for kind, axis, rows in KINDS:
        for k, (way, o, n) in enumerate(rows):
            after = {"zy": tuple(("z", i) for i in range(4)), "yz": (("y", k),)}.get(kind, ())
            specs.append(((kind, k), axis, way, n * HALF * 4 * (NZ if kind == "y" else 1), after))
    return specs


def finish_plan():
    specs = {s[0]: s for s in stream_specs()}
    free, heap, plan, count, ended = {}, [], [], 0, set()

    def wire(now, axis, way, size):
        end = max(now, free.get((axis, way), 0.0)) + size / RATE
        free[axis, way] = end
        return end + HOP

    def post(when, what):
        nonlocal count
        count += 1
        heapq.heappush(heap, (when, count, what))

    def begin(now, name):
        _, axis, way, size, _ = specs[name]
        post(wire(now, axis, way, size), ("serve", name, 0))

    def gram_sends(now, stage):
        q = SLOTS * B * B * 4 // NZ
        if stage in (0, 2):
            when = max(wire(now, "z", way, 8 * q) for way in (1, -1)) + 1.5 * HOP
        elif stage == 1:
            when = max(wire(now, "y", way, 2 * q) for way in (1, -1)) + HOP
        else:
            when = now + (11.0 if stage == 3 else 3.5)
        post(when, ("gram", stage + 1))

    now = 1.5
    gram_sends(now, 0)
    now += 3.0
    zfirst = [n for n, s in specs.items() if not s[4] and s[1] == "z"]
    yfirst = [n for n, s in specs.items() if not s[4] and s[1] == "y"]
    early = zfirst[0:3:2]
    held = {1: yfirst, 2: [n for n in zfirst if n not in early]}

    def launch(names):
        for name in names:
            begin(now, name)
        plan.append(("begin", names))

    launch(early)
    plan.append(("tiles",))
    now += 3.4
    chol = []
    while heap or chol:
        if heap and (heap[0][0] <= now or not chol):
            when, _, what = heapq.heappop(heap)
            now = max(now, when)
            plan.append(what)
            if what[0] == "gram":
                now += 0.3
                if what[1] < 5:
                    gram_sends(now, what[1])
                    launch(held.get(what[1], []))
                else:
                    now += 1.0
                    chol = [c for b in range(6) for c in [("chol", b, p) for p in range(4)] + [("block", b)]]
            else:
                _, name, s = what
                _, axis, way, size, _ = specs[name]
                now += 0.1 + size / 3e6
                if s < SIZES[axis] - 2:
                    post(wire(now, axis, way, size), ("serve", name, s + 1))
                else:
                    ended.add(name)
                    for other, spec in specs.items():
                        if name in spec[4] and all(x in ended for x in spec[4]):
                            begin(now, other)
                            plan.append(("begin", [other]))
        else:
            what = chol.pop(0)
            plan.append(what)
            now += 1.35 if what[0] == "chol" else 2.0
            chol_end = now
    return plan, now, chol_end


class Stream:
    def __init__(self, axis, way, local, buf, sink, sems, base):
        self.axis, self.way, self.n = axis, way, SIZES[axis]
        self.local, self.buf, self.sink, self.sems, self.base = local, buf, sink, sems, base

    def block(self, back):
        n = self.n
        return lax.rem(lax.axis_index(self.axis) + (2 * n - back if self.way == 1 else back), n)

    def copy(self, s):
        return pltpu.make_async_remote_copy(
            src_ref=self.local(self.block(1)) if s == 0 else self.buf.at[s - 1],
            dst_ref=self.buf.at[s],
            send_sem=self.sems[0].at[self.base + s], recv_sem=self.sems[1].at[self.base + s],
            device_id={self.axis: step_to(self.axis, 1 if self.way == 1 else self.n - 1)}, device_id_type=MESH,
        )

    def serve(self, s):
        self.copy(s).wait_recv()
        total = self.buf[s] + self.local(self.block(2 + s))[...]
        if s < self.n - 2:
            self.buf[s] = total
            self.copy(s + 1).start()
        else:
            self.sink[...] = total

    def finish(self):
        for s in range(self.n - 1):
            self.copy(s).wait_send()


def sub_start(i):
    return pl.multiple_of(i * 140 // 8 * 8, 8)


RS_COPIES = 4 * 7 + 4 * 3 + 2 * 3 + 4 * 7


def finish_kernel(slab, s, out, w, c, resz, resy, *rest):
    zb, yb, zyb, yzb = rest[0:4], rest[4:8], rest[8:10], rest[10:14]
    hi, lo, gp, gz, own, gy, full, a, lfac, m, v, ss, rs, gs, gr = rest[14:]
    sems = (ss, rs)
    tiles = slab.shape[1] // B
    greet(GRAM_PEERS)
    exchange = gram_exchange(gp, gz, own, gy, full, (gs, gr), 0)
    gram_compute(s, gp)
    next(exchange)
    for k in range(s.shape[0] // B):
        turned = s[k * B:(k + 1) * B, :].T
        top = turned.astype(jnp.bfloat16)
        hi[:, k * B:(k + 1) * B] = top
        lo[:, k * B:(k + 1) * B] = (turned - top.astype(F32)).astype(jnp.bfloat16)

    def tile(t, _):
        part = slab[:, pl.ds(pl.multiple_of(t * B, B), B)]
        value = lax.dot_general(part, hi[...], (TN, ((), ())), preferred_element_type=F32)
        value = value + lax.dot_general(part, lo[...], (TN, ((), ())), preferred_element_type=F32)
        for k in range(8):
            q = t * 8 + k
            c[q // 35, pl.ds(pl.multiple_of(lax.rem(q, 35) * 16, 16), 16), :] = value[k * 16:(k + 1) * 16, :]
        return 0

    start = lax.rem(lax.axis_index("z") + NZ - 1, NZ) * (slab.shape[1] // NZ) // B
    early = 15

    def tiles_of(lo, hi):
        lax.fori_loop(lo, hi, lambda t, _: tile(lax.rem(start + t, tiles), 0), 0)

    streams, base = {}, 0
    for kind, axis, rows in KINDS:
        for k, (way, o, n) in enumerate(rows):
            buf, sink = {
                "z": lambda: (zb[k], resz.at[o:o + n]),
                "y": lambda: (yb[k], resy.at[:, o:o + n]),
                "zy": lambda: (zyb[k], out.at[o:o + n, 0:HALF]),
                "yz": lambda: (yzb[k], out.at[o:o + n, HALF:2 * HALF]),
            }[kind]()
            local = functools.partial(lambda i, kind, o, n: {
                "z": lambda: c.at[i, o:o + n, 0:HALF],
                "y": lambda: c.at[:, pl.ds(sub_start(i) + o, n), HALF:2 * HALF],
                "zy": lambda: resz.at[pl.ds(sub_start(i) + o, n)],
                "yz": lambda: resy.at[i, o:o + n],
            }[kind](), kind=kind, o=o, n=n)
            streams[kind, k] = Stream(axis, way, local, buf, sink, sems, base)
            base += SIZES[axis] - 1

    n = 6

    def act(what):
        if what[0] == "gram":
            next(exchange, None)
            if what[1] == 5:
                for i in range(n):
                    for j in range(i + 1):
                        t = i * (i + 1) // 2 + j
                        a[i * B:(i + 1) * B, j * B:(j + 1) * B] = full[t // 6, t // 3 % 2, (t % 3) * B:(t % 3 + 1) * B, :]
        elif what[0] == "begin":
            for name in what[1]:
                streams[name].copy(0).start()
        elif what[0] == "serve":
            streams[what[1]].serve(what[2])
        elif what[0] == "tiles":
            tiles_of(early, tiles)

    plan = finish_plan()[0]
    first = next(i for i, what in enumerate(plan) if what[0] == "chol")
    last = max(i for i, what in enumerate(plan) if what[0] == "block")
    table, key = {}, None
    for what in plan[first:last + 1]:
        if what[0] == "chol":
            key = what[1], what[2]
        elif what[0] == "block":
            key = what[1], 4
        else:
            table.setdefault(key, []).append(what)

    tiles_of(0, early)
    w[...] = jnp.zeros_like(w)
    for what in plan[:first]:
        act(what)
    row_of = lax.broadcasted_iota(jnp.int32, (B, B), 0)
    col_of = lax.broadcasted_iota(jnp.int32, (B, B), 1)
    eye = jnp.where(row_of == col_of, 1.0, 0.0).astype(F32)

    def step(b, _):
        o = pl.multiple_of(b * B, B)
        m[:, :B] = a[pl.ds(o, B), pl.ds(o, B)]
        m[:, B:] = eye
        for piece in range(5):
            if piece < 4:
                factor_panels(m, v, 4 * piece, 4 * piece + 4)
            for k in range(n):
                if piece == 4 or table.get((k, piece)):
                    @pl.when(b == k)
                    def _():
                        if piece == 4:
                            chol_block(a, w, lfac, m, v, k)
                        for what in table.get((k, piece), ()):
                            act(what)
        return 0

    lax.fori_loop(0, n, step, 0)
    for what in plan[last + 1:]:
        act(what)
    for stream in streams.values():
        stream.finish()


def finish(slab, s):
    bf = jnp.bfloat16
    C, R = s.shape
    vm = lambda *shape: pltpu.VMEM(shape, F32)
    return pl.pallas_call(
        finish_kernel,
        out_shape=(jax.ShapeDtypeStruct((144, C), F32), jax.ShapeDtypeStruct((C, C), F32)),
        in_specs=[VM, VM], out_specs=(VM, VM),
        scratch_shapes=[
            vm(NZ, 560, C), vm(560, HALF), vm(NZ, 144, HALF),
            *[vm(NZ - 1, n, HALF) for _, _, n in Z_ROWS],
            *[vm(NY - 1, NZ, n, HALF) for _, _, n in Y_ROWS],
            *[vm(NY - 1, n, HALF) for _, _, n in ZY_ROWS],
            *[vm(NZ - 1, n, HALF) for _, _, n in Y_ROWS],
            pltpu.VMEM((R, C), bf), pltpu.VMEM((R, C), bf),
            *GRAM_SCRATCH, vm(NX, 2, SLOTS * B, B), vm(C, C), vm(C, C), vm(B, 2 * B), vm(B, B),
            DMA((RS_COPIES,)), DMA((RS_COPIES,)), DMA((GRAM_COPIES,)), DMA((GRAM_COPIES,)),
        ],
        compiler_params=pltpu.CompilerParams(collective_id=2, has_side_effects=True, vmem_limit_bytes=60 * 2**20), name="finish",
    )(slab, s)


def body(slab, test):
    c, w = finish(slab, sketch_of(test.T, slab))
    y = lax.axis_index("y")
    c = lax.dynamic_slice_in_dim(c, y * 140 % 8, 140, 0)
    p = lax.dot_general(w, c, (NT, ((), ())), precision=HI, preferred_element_type=F32)
    p = lax.all_to_all(p.reshape(NZ * NY, 24, -1), ("z", "y"), 0, 0, tiled=True)
    return p.transpose(1, 0, 2).reshape(24, -1)


def solution(mesh):
    split = Mesh(mesh.devices.reshape(NZ, NY, NX, 2), AXES)
    return jax.shard_map(
        body, mesh=split, in_specs=(P(("z", "y"), ("x", "c")), P(("x", "c"), ("z", "y"))),
        out_specs=P(("z", "y"), ("x", "c")), check_vma=False,
    )
```

```python
import functools
import heapq
import jax, jax.numpy as jnp
from jax import lax
from jax.experimental import pallas as pl
from jax.experimental.pallas import tpu as pltpu
from jax.sharding import Mesh
from jax.sharding import PartitionSpec as P
HI = lax.Precision.HIGHEST
F32 = jnp.float32
B = 128

def dot(x, y, dims, precision=HI):
    return lax.dot_general(x, y, (dims, ((), ())), precision=precision, preferred_element_type=F32)
NN = ((1,), (0,)); NT = ((1,), (1,)); TN = ((0,), (0,))

def lanes(x, j): return jnp.broadcast_to(x[:, j:j + 1], (x.shape[0], 128))
def row(x, j): return jnp.broadcast_to(x[j:j + 1, :], (8, 128))

def factor_panels(m, v, lo, hi):
    sub = lax.broadcasted_iota(jnp.int32, (8, 128), 0)
    for t in range(lo, hi):
        k = 8 * t
        left, right = m[k:k + 8, :128], m[k:k + 8, 128:]
        cols = [lanes(left, k + j) for j in range(8)]
        d = {(i, j): row(cols[j], i) for i in range(8) for j in range(i + 1)}
        l, inv = {}, []
        for j in range(8):
            r = lax.rsqrt(d[j, j])
            inv.append(r)
            for i in range(j + 1, 8):
                l[i, j] = d[i, j] * r
            for i in range(j + 1, 8):
                for h in range(j + 1, i + 1):
                    d[i, h] = d[i, h] - l[i, j] * l[h, j]
        rows = []
        for part in (left, right):
            raw = [row(part, i) for i in range(8)]
            done = []
            for i in range(8):
                x = raw[i]
                for j in range(i):
                    x = x - l[i, j] * done[j]
                done.append(x * inv[i])
            rows.append(done)
        tile = rows[1][0]
        for i in range(1, 8):
            tile = jnp.where(sub == i, rows[1][i], tile)
        v[k:k + 8, :] = tile
        if t < 15:
            q = []
            for done in rows:
                back = [None] * 8
                for i in reversed(range(8)):
                    x = done[i]
                    for j in range(i + 1, 8):
                        x = x - l[j, i] * back[j]
                    back[i] = x * inv[i]
                q.append(back)
            e = k + 8
            ml, mr = m[e:, :128], m[e:, 128:]
            al, ar = ml, mr
            for i in range(8):
                c = jnp.broadcast_to(ml[:, k + i:k + i + 1], ml.shape)
                al = al - c * q[0][i][:1, :]
                ar = ar - c * q[1][i][:1, :]
            m[e:, :128] = al
            m[e:, 128:] = ar

def chol_block(a, w, lfac, m, v, b, n=6):
    s, e = b * B, (b + 1) * B
    vb = v[...]
    w[s:e, s:e] = vb
    if b:
        part = dot(lfac[s:e, :s], w[:s, :s], NN)
        w[s:e, :s] = -dot(vb, part, NN)
    if b < n - 1:
        lfac[e:, s:e] = dot(a[e:, s:e], vb, NT)
        for j in range(b + 1, n):
            js, je = j * B, (j + 1) * B
            a[js:, js:je] = a[js:, js:je] - dot(lfac[js:, s:e], lfac[js:je, s:e], NT)

MESH = pl.DeviceIdType.MESH
NZ, NY, NX = 8, 4, 4
AXES = ("z", "y", "x", "c")
SIZES = {"z": NZ, "y": NY, "x": NX, "c": 2}
VM = pl.BlockSpec(memory_space=pltpu.VMEM)
ANY = pl.BlockSpec(memory_space=pl.ANY)
DMA = pltpu.SemaphoreType.DMA


def step_to(axis, hops):
    return lax.rem(lax.axis_index(axis) + hops, SIZES[axis])


def greet(peers):
    barrier = pltpu.get_barrier_semaphore()
    for axis, hops in peers:
        pl.semaphore_signal(barrier, inc=1, device_id={axis: step_to(axis, hops)}, device_id_type=MESH)
    pl.semaphore_wait(barrier, len(peers))


def send(src, dst, sems, k, axis, hops):
    copy = pltpu.make_async_remote_copy(
        src_ref=src, dst_ref=dst, send_sem=sems[0].at[k], recv_sem=sems[1].at[k],
        device_id={axis: step_to(axis, hops)}, device_id_type=MESH,
    )
    copy.start()
    return copy


RATE, HOP = 42e3, 2.0


def sketch_plan(d, cut, K):
    free, heap, plan, count, order = {}, [], [], 0, 0
    missing = {dz: NY * K for dz in range(NZ)}

    def post(when, what):
        nonlocal order
        order += 1
        heapq.heappush(heap, (when, order, what))

    def start(now, phase, way, step, dz, dy, lo, hi):
        nonlocal count
        axis = phase[1]
        end = max(now, free.get((axis, way), 0.0)) + d * (hi - lo) * 2 / RATE
        free[axis, way] = end
        job = (phase, axis, way, step, dz, dy, lo, hi, count)
        count += 1
        post(end + HOP, ("got", job))
        return job

    def both(now, phase, dz, dy, lo, hi):
        return [start(now, phase, way, 0, dz, dy, lo, hi) for way in (1, -1)]

    def share(now, axis, size, lag):
        end = max(now, free.get(axis, 0.0)) + size / (100e3 if axis == "c" else RATE / 2)
        free[axis] = end
        return end + lag

    first = both(0, "ly", 0, 0, 0, cut) + both(0, "rz", 0, 0, cut, K)
    first += both(0, "lz", 0, 0, 0, cut) + both(0, "ry", 0, 0, cut, K)
    plan.append(("got", None, first))
    missing[0] -= K
    now = 0.0
    rows = NY * d
    while heap:
        when, _, what = heapq.heappop(heap)
        now = max(now, when) + 0.05
        if what[0] == "got":
            job = what[1]
            phase, axis, way, step, dz, dy, lo, hi, _ = job
            dz, dy = (dz - way, dy) if axis == "z" else (dz, dy - way)
            mid = lo + ((hi - lo) // 128 + 1) // 2 * 128
            far = SIZES[axis] // 2
            new = []
            if step < far - 1:
                a, b = (lo, hi) if step < far - 2 else ((lo, mid) if way == 1 else (mid, hi))
                if b > a:
                    new.append(start(now, phase, way, step + 1, dz, dy, a, b))
            if phase in ("ly", "rz"):
                new += both(now, "lz" if phase == "ly" else "ry", dz, dy, lo, hi)
            plan.append(("got", job, new))
            missing[dz % NZ] -= hi - lo
            if not missing[dz % NZ]:
                post(now + 0.3, ("product", dz % NZ))
        elif what[0] == "product":
            plan.append(what)
            now += 1.5
            post(share(now, "c", rows * 512, 1.5), ("sum", what[1], 1))
        else:
            _, dz, stage = what
            plan.append(what)
            now += 0.2
            if stage == 1:
                post(share(now, "x", rows * 512, HOP + 1), ("sum", dz, 2))
            elif stage == 2:
                post(share(now, "c", rows * 512, 1.5), ("sum", dz, 3))
    return plan, count, now


def sketch_part(plan, t, slab, slab_copy, st, g, part, near, acc, far, gs, gr, ss, sr, own_sem):
    z, y, x, c = (lax.axis_index(axis) for axis in AXES)
    d = t.shape[0] * 8
    rows = NY * d
    half = st.shape[1] // 2

    def place(dz, dy, lo, hi):
        at = (lax.rem(z + dz + NZ, NZ) * NY + lax.rem(y + dy + NY, NY)) * d
        return g.at[pl.ds(at // 8, d // 8), :, lo:hi]

    def copy(job):
        phase, axis, way, step, dz, dy, lo, hi, k = job
        to = place(dz, dy, lo, hi)
        return pltpu.make_async_remote_copy(
            src_ref=t.at[:, :, lo:hi] if dz == dy == 0 else to, dst_ref=to, send_sem=gs.at[k], recv_sem=gr.at[k],
            device_id={axis: step_to(axis, 1 if way == 1 else SIZES[axis] - 1)}, device_id_type=MESH,
        )

    def rows_of(dz):
        return pl.multiple_of(lax.rem(z + dz, NZ) * rows, 8)

    def lanes_of(core):
        return pl.ds(pl.multiple_of(core * half, half), half)

    def remote(src, dst, k, axis, hops):
        return pltpu.make_async_remote_copy(
            src_ref=src, dst_ref=dst, send_sem=ss.at[k], recv_sem=sr.at[k],
            device_id={axis: step_to(axis, hops)}, device_id_type=MESH,
        )

    def exchange(dz, stage):
        k = dz * 5
        if stage == 1:
            return [remote(part.at[dz, :, lanes_of(1 - c)], near.at[dz], k, "c", 1)]
        if stage == 2:
            return [remote(acc.at[dz], far.at[dz, x], k + i, "x", i) for i in (1, 2, 3)]
        all_mine = st.at[pl.ds(rows_of(dz), rows), lanes_of(c)]
        return [remote(all_mine, all_mine, k + 4, "c", 1)]

    def begin(dz, stage):
        for one in exchange(dz, stage):
            one.start()

    keep = pltpu.make_async_copy(t, place(0, 0, 0, t.shape[2]), own_sem)
    kept = False
    for what in plan:
        if what[0] == "got":
            if what[1] is not None:
                copy(what[1]).wait_recv()
            for job in what[2]:
                copy(job).start()
            if what[1] is None:
                keep.start()
        elif what[0] == "product":
            dz = what[1]
            if not kept:
                keep.wait()
                slab_copy.wait()
                kept = True
            part[dz] = lax.dot_general(g[pl.ds(rows_of(dz) // 8, rows // 8)].reshape(rows, g.shape[2]), slab[...], (NT, ((), ())), preferred_element_type=F32)
            begin(dz, 1)
        else:
            _, dz, stage = what
            for one in exchange(dz, stage):
                one.wait_recv()
            if stage == 1:
                total = part[dz, :, lanes_of(c)] + near[dz]
                acc[dz] = total
                far[dz, x] = total
            elif stage == 2:
                total = far[dz, 0]
                for other in range(1, NX):
                    total = total + far[dz, other]
                st[pl.ds(rows_of(dz), rows), lanes_of(c)] = total
            if stage < 3:
                begin(dz, stage + 1)
    for what in plan:
        if what[0] == "got" and what[1] is not None:
            copy(what[1]).wait_send()
        elif what[0] == "sum":
            for one in exchange(what[1], what[2]):
                one.wait_send()


SLOTS = 3


def place(t):
    at_least = lambda k: (t + 32 - k) // 32
    i = at_least(1) + at_least(3) + at_least(6) + at_least(10) + at_least(15)
    j = t - i * (i + 1) // 2
    spare = at_least(21)
    return i, j * (1 - spare)


def gram_compute(s, gp):
    a = lax.axis_index("x") * 2 + lax.axis_index("c")
    for k in range(SLOTS):
        i, j = place(a * SLOTS + k)
        li = s[pl.ds(pl.multiple_of(i * B, B), B), :]
        lj = s[pl.ds(pl.multiple_of(j * B, B), B), :]
        gp[k * B:(k + 1) * B, :] = dot(li, lj, NT)


GRAM_PEERS = [("z", i) for i in range(1, NZ)] + [("y", i) for i in range(1, NY)] + [("x", i) for i in range(1, NX)] + [("c", 1)]
GRAM_COPIES = 7 + 3 + 7 + 3 + 1


def gram_exchange(gp, gz, own, gy, full, sems, base):
    x, c, z = lax.axis_index("x"), lax.axis_index("c"), lax.axis_index("z")
    q = gp.shape[0] // NZ
    copies = []
    ones = []
    for i in range(1, NZ):
        o = pl.multiple_of(step_to("z", i) * q, q)
        ones.append(send(gp.at[pl.ds(o, q)], gz.at[i - 1], sems, base + i - 1, "z", i))
    yield
    mine = pl.ds(pl.multiple_of(z * q, q), q)
    total = gp[mine, :]
    for i in range(1, NZ):
        ones[i - 1].wait_recv()
        total = total + gz[i - 1]
    own[...] = total
    twos = [send(own, gy.at[i - 1], sems, base + 6 + i, "y", i) for i in range(1, NY)]
    yield
    total = own[...]
    for i in range(1, NY):
        twos[i - 1].wait_recv()
        total = total + gy[i - 1]
    full[x, c, mine, :] = total
    here = full.at[x, c, mine]
    threes = [send(here, here, sems, base + 9 + i, "z", i) for i in range(1, NZ)]
    yield
    for t in threes:
        t.wait_recv()
    all_mine = full.at[x, c]
    fours = [send(all_mine, all_mine, sems, base + 16 + i, "x", i) for i in range(1, NX)]
    yield
    for t in fours:
        t.wait_recv()
    column = full.at[:, c]
    five = send(column, column, sems, base + 20, "c", 1)
    yield
    five.wait_recv()
    for t in (*ones, *twos, *threes, *fours, five):
        t.wait_send()


GRAM_SCRATCH = [pltpu.VMEM((SLOTS * B, B), F32), pltpu.VMEM((NZ - 1, SLOTS * B // NZ, B), F32), pltpu.VMEM((SLOTS * B // NZ, B), F32), pltpu.VMEM((NY - 1, SLOTS * B // NZ, B), F32)]


Z_ROWS = ((1, 0, 144), (1, 144, 136), (-1, 280, 144), (-1, 424, 136))
Y_ROWS = ((1, 0, 40), (1, 40, 32), (-1, 72, 40), (-1, 112, 32))
ZY_ROWS = ((1, 0, 72), (-1, 72, 72))
HALF = 384
KINDS = (("z", "z", Z_ROWS), ("y", "y", Y_ROWS), ("zy", "y", ZY_ROWS), ("yz", "z", Y_ROWS))


def stream_specs():
    specs = []
    for kind, axis, rows in KINDS:
        for k, (way, o, n) in enumerate(rows):
            after = {"zy": tuple(("z", i) for i in range(4)), "yz": (("y", k),)}.get(kind, ())
            specs.append(((kind, k), axis, way, n * HALF * 4 * (NZ if kind == "y" else 1), after))
    return specs


def finish_plan():
    specs = {s[0]: s for s in stream_specs()}
    free, heap, plan, count, ended = {}, [], [], 0, set()

    def wire(now, axis, way, size):
        end = max(now, free.get((axis, way), 0.0)) + size / RATE
        free[axis, way] = end
        return end + HOP

    def post(when, what):
        nonlocal count
        count += 1
        heapq.heappush(heap, (when, count, what))

    def begin(now, name):
        _, axis, way, size, _ = specs[name]
        post(wire(now, axis, way, size), ("serve", name, 0))

    def gram_sends(now, stage):
        q = SLOTS * B * B * 4 // NZ
        if stage in (0, 2):
            when = max(wire(now, "z", way, 8 * q) for way in (1, -1)) + 1.5 * HOP
        elif stage == 1:
            when = max(wire(now, "y", way, 2 * q) for way in (1, -1)) + HOP
        else:
            when = now + (11.0 if stage == 3 else 3.5)
        post(when, ("gram", stage + 1))

    now = 1.5
    gram_sends(now, 0)
    now += 3.0
    zfirst = [n for n, s in specs.items() if not s[4] and s[1] == "z"]
    yfirst = [n for n, s in specs.items() if not s[4] and s[1] == "y"]
    early = zfirst[0:3:2]
    held = {1: yfirst, 2: [n for n in zfirst if n not in early]}

    def launch(names):
        for name in names:
            begin(now, name)
        plan.append(("begin", names))

    launch(early)
    plan.append(("tiles",))
    now += 3.4
    chol = []
    while heap or chol:
        if heap and (heap[0][0] <= now or not chol):
            when, _, what = heapq.heappop(heap)
            now = max(now, when)
            plan.append(what)
            if what[0] == "gram":
                now += 0.3
                if what[1] < 5:
                    gram_sends(now, what[1])
                    launch(held.get(what[1], []))
                else:
                    now += 1.0
                    chol = [c for b in range(6) for c in [("chol", b, p) for p in range(4)] + [("block", b)]]
            else:
                _, name, s = what
                _, axis, way, size, _ = specs[name]
                now += 0.1 + size / 3e6
                if s < SIZES[axis] - 2:
                    post(wire(now, axis, way, size), ("serve", name, s + 1))
                else:
                    ended.add(name)
                    for other, spec in specs.items():
                        if name in spec[4] and all(x in ended for x in spec[4]):
                            begin(now, other)
                            plan.append(("begin", [other]))
        else:
            what = chol.pop(0)
            plan.append(what)
            now += 1.35 if what[0] == "chol" else 2.0
            chol_end = now
    return plan, now, chol_end


class Stream:
    def __init__(self, axis, way, local, buf, sink, sems, base):
        self.axis, self.way, self.n = axis, way, SIZES[axis]
        self.local, self.buf, self.sink, self.sems, self.base = local, buf, sink, sems, base

    def block(self, back):
        n = self.n
        return lax.rem(lax.axis_index(self.axis) + (2 * n - back if self.way == 1 else back), n)

    def copy(self, s):
        return pltpu.make_async_remote_copy(
            src_ref=self.local(self.block(1)) if s == 0 else self.buf.at[s - 1],
            dst_ref=self.buf.at[s],
            send_sem=self.sems[0].at[self.base + s], recv_sem=self.sems[1].at[self.base + s],
            device_id={self.axis: step_to(self.axis, 1 if self.way == 1 else self.n - 1)}, device_id_type=MESH,
        )

    def serve(self, s):
        self.copy(s).wait_recv()
        total = self.buf[s] + self.local(self.block(2 + s))[...]
        if s < self.n - 2:
            self.buf[s] = total
            self.copy(s + 1).start()
        else:
            self.sink[...] = total

    def finish(self):
        for s in range(self.n - 1):
            self.copy(s).wait_send()


def sub_start(i):
    return pl.multiple_of(i * 140 // 8 * 8, 8)


RS_COPIES = 4 * 7 + 4 * 3 + 2 * 3 + 4 * 7


def whole_kernel(plan, t, slab_in, p, slab, slab_sem, st, g, part, near, acc, far, ts, tr, us, ur, own_sem, *rest):
    out, w, c, resz, resy = rest[:5]
    rest = rest[5:]
    zb, yb, zyb, yzb = rest[0:4], rest[4:8], rest[8:10], rest[10:14]
    hi, lo, gp, gz, own, gy, full, a, lfac, m, v, ss, rs, gs, gr = rest[14:]
    slab_copy = pltpu.make_async_copy(slab_in, slab, slab_sem)
    slab_copy.start()
    greet(GRAM_PEERS)
    sketch_part(plan, t, slab, slab_copy, st, g, part, near, acc, far, ts, tr, us, ur, own_sem)
    s = st
    sems = (ss, rs)
    tiles = slab.shape[1] // B
    exchange = gram_exchange(gp, gz, own, gy, full, (gs, gr), 0)
    gram_compute(s, gp)
    next(exchange)
    for k in range(s.shape[0] // B):
        turned = s[k * B:(k + 1) * B, :].T
        top = turned.astype(jnp.bfloat16)
        hi[:, k * B:(k + 1) * B] = top
        lo[:, k * B:(k + 1) * B] = (turned - top.astype(F32)).astype(jnp.bfloat16)

    def tile(t, _):
        part = slab[:, pl.ds(pl.multiple_of(t * B, B), B)]
        value = lax.dot_general(part, hi[...], (TN, ((), ())), preferred_element_type=F32)
        value = value + lax.dot_general(part, lo[...], (TN, ((), ())), preferred_element_type=F32)
        for k in range(8):
            q = t * 8 + k
            c[q // 35, pl.ds(pl.multiple_of(lax.rem(q, 35) * 16, 16), 16), :] = value[k * 16:(k + 1) * 16, :]
        return 0

    start = lax.rem(lax.axis_index("z") + NZ - 1, NZ) * (slab.shape[1] // NZ) // B
    early = 15

    def tiles_of(lo, hi):
        lax.fori_loop(lo, hi, lambda t, _: tile(lax.rem(start + t, tiles), 0), 0)

    streams, base = {}, 0
    for kind, axis, rows in KINDS:
        for k, (way, o, n) in enumerate(rows):
            buf, sink = {
                "z": lambda: (zb[k], resz.at[o:o + n]),
                "y": lambda: (yb[k], resy.at[:, o:o + n]),
                "zy": lambda: (zyb[k], out.at[o:o + n, 0:HALF]),
                "yz": lambda: (yzb[k], out.at[o:o + n, HALF:2 * HALF]),
            }[kind]()
            local = functools.partial(lambda i, kind, o, n: {
                "z": lambda: c.at[i, o:o + n, 0:HALF],
                "y": lambda: c.at[:, pl.ds(sub_start(i) + o, n), HALF:2 * HALF],
                "zy": lambda: resz.at[pl.ds(sub_start(i) + o, n)],
                "yz": lambda: resy.at[i, o:o + n],
            }[kind](), kind=kind, o=o, n=n)
            streams[kind, k] = Stream(axis, way, local, buf, sink, sems, base)
            base += SIZES[axis] - 1

    n = 6

    def act(what):
        if what[0] == "gram":
            next(exchange, None)
            if what[1] == 5:
                for i in range(n):
                    for j in range(i + 1):
                        t = i * (i + 1) // 2 + j
                        a[i * B:(i + 1) * B, j * B:(j + 1) * B] = full[t // 6, t // 3 % 2, (t % 3) * B:(t % 3 + 1) * B, :]
        elif what[0] == "begin":
            for name in what[1]:
                streams[name].copy(0).start()
        elif what[0] == "serve":
            streams[what[1]].serve(what[2])
        elif what[0] == "tiles":
            tiles_of(early, tiles)

    plan = finish_plan()[0]
    first = next(i for i, what in enumerate(plan) if what[0] == "chol")
    last = max(i for i, what in enumerate(plan) if what[0] == "block")
    table, key = {}, None
    for what in plan[first:last + 1]:
        if what[0] == "chol":
            key = what[1], what[2]
        elif what[0] == "block":
            key = what[1], 4
        else:
            table.setdefault(key, []).append(what)

    tiles_of(0, early)
    w[...] = jnp.zeros_like(w)
    for what in plan[:first]:
        act(what)
    row_of = lax.broadcasted_iota(jnp.int32, (B, B), 0)
    col_of = lax.broadcasted_iota(jnp.int32, (B, B), 1)
    eye = jnp.where(row_of == col_of, 1.0, 0.0).astype(F32)

    def step(b, _):
        o = pl.multiple_of(b * B, B)
        m[:, :B] = a[pl.ds(o, B), pl.ds(o, B)]
        m[:, B:] = eye
        for piece in range(5):
            if piece < 4:
                factor_panels(m, v, 4 * piece, 4 * piece + 4)
            for k in range(n):
                if piece == 4 or table.get((k, piece)):
                    @pl.when(b == k)
                    def _():
                        if piece == 4:
                            chol_block(a, w, lfac, m, v, k)
                        for what in table.get((k, piece), ()):
                            act(what)
        return 0

    lax.fori_loop(0, n, step, 0)
    for what in plan[last + 1:]:
        act(what)
    odd = lax.rem(lax.axis_index("y"), 2)
    mine = p.shape[1]
    skip = out.shape[0] - mine
    share = jnp.where(odd == 1, out[skip:, :], out[:mine, :])
    for b in range(n):
        e = (b + 1) * B
        p[b * B:e, :] = dot(w[b * B:e, :e], share[:, :e], NT)
    for stream in streams.values():
        stream.finish()


def whole(t, slab):
    d, K = t.shape
    R = slab.shape[0]
    plan, count, _ = sketch_plan(d, K // 128 * 2 // 5 * 128, K)
    C, rows = NZ * NY * d, NY * d
    bf = jnp.bfloat16
    vm = lambda *shape: pltpu.VMEM(shape, F32)
    HBM = pl.BlockSpec(memory_space=pltpu.HBM)
    return pl.pallas_call(
        functools.partial(whole_kernel, plan),
        out_shape=jax.ShapeDtypeStruct((C, K // (NZ * NY)), F32),
        in_specs=[HBM, HBM], out_specs=VM,
        scratch_shapes=[
            pltpu.VMEM((R, K), bf), DMA, vm(C, R), pltpu.VMEM((C // 8, 8, K), bf),
            vm(NZ, rows, R), vm(NZ, rows, R // 2), vm(NZ, rows, R // 2), vm(NZ, NX, rows, R // 2),
            DMA((count,)), DMA((count,)), DMA((40,)), DMA((40,)), DMA,
            vm(144, C), vm(C, C),
            vm(NZ, 560, C), vm(560, HALF), vm(NZ, 144, HALF),
            *[vm(NZ - 1, n, HALF) for _, _, n in Z_ROWS],
            *[vm(NY - 1, NZ, n, HALF) for _, _, n in Y_ROWS],
            *[vm(NY - 1, n, HALF) for _, _, n in ZY_ROWS],
            *[vm(NZ - 1, n, HALF) for _, _, n in Y_ROWS],
            pltpu.VMEM((R, C), bf), pltpu.VMEM((R, C), bf),
            *GRAM_SCRATCH, vm(NX, 2, SLOTS * B, B), vm(C, C), vm(C, C), vm(B, 2 * B), vm(B, B),
            DMA((RS_COPIES,)), DMA((RS_COPIES,)), DMA((GRAM_COPIES,)), DMA((GRAM_COPIES,)),
        ],
        compiler_params=pltpu.CompilerParams(collective_id=0, has_side_effects=True, vmem_limit_bytes=63 * 2**20), name="whole",
    )(t.reshape(d // 8, 8, K), slab)


def body(slab, test):
    p = whole(test.T, slab)
    p = lax.all_to_all(p.reshape(NZ * NY, 24, -1), ("z", "y"), 0, 0, tiled=True)
    return p.transpose(1, 0, 2).reshape(24, -1)


def solution(mesh):
    split = Mesh(mesh.devices.reshape(NZ, NY, NX, 2), AXES)
    return jax.shard_map(
        body, mesh=split, in_specs=(P(("z", "y"), ("x", "c")), P(("x", "c"), ("z", "y"))),
        out_specs=P(("z", "y"), ("x", "c")), check_vma=False,
    )
```

```python
import functools
import heapq
import jax, jax.numpy as jnp
from jax import lax
from jax.experimental import pallas as pl
from jax.experimental.pallas import tpu as pltpu
from jax.sharding import Mesh
from jax.sharding import PartitionSpec as P
HI = lax.Precision.HIGHEST
F32 = jnp.float32
B = 128

def dot(x, y, dims, precision=HI):
    return lax.dot_general(x, y, (dims, ((), ())), precision=precision, preferred_element_type=F32)
NN = ((1,), (0,)); NT = ((1,), (1,)); TN = ((0,), (0,))

def lanes(x, j): return jnp.broadcast_to(x[:, j:j + 1], (x.shape[0], 128))
def row(x, j): return jnp.broadcast_to(x[j:j + 1, :], (8, 128))

def factor_panels(m, v, lo, hi):
    sub = lax.broadcasted_iota(jnp.int32, (8, 128), 0)
    for t in range(lo, hi):
        k = 8 * t
        left, right = m[k:k + 8, :128], m[k:k + 8, 128:]
        cols = [lanes(left, k + j) for j in range(8)]
        d = {(i, j): row(cols[j], i) for i in range(8) for j in range(i + 1)}
        l, inv = {}, []
        for j in range(8):
            r = lax.rsqrt(d[j, j])
            inv.append(r)
            for i in range(j + 1, 8):
                l[i, j] = d[i, j] * r
            for i in range(j + 1, 8):
                for h in range(j + 1, i + 1):
                    d[i, h] = d[i, h] - l[i, j] * l[h, j]
        rows = []
        for part in (left, right):
            raw = [row(part, i) for i in range(8)]
            done = []
            for i in range(8):
                x = raw[i]
                for j in range(i):
                    x = x - l[i, j] * done[j]
                done.append(x * inv[i])
            rows.append(done)
        tile = rows[1][0]
        for i in range(1, 8):
            tile = jnp.where(sub == i, rows[1][i], tile)
        v[k:k + 8, :] = tile
        if t < 15:
            q = []
            for done in rows:
                back = [None] * 8
                for i in reversed(range(8)):
                    x = done[i]
                    for j in range(i + 1, 8):
                        x = x - l[j, i] * back[j]
                    back[i] = x * inv[i]
                q.append(back)
            e = k + 8
            ml, mr = m[e:, :128], m[e:, 128:]
            al, ar = ml, mr
            for i in range(8):
                c = jnp.broadcast_to(ml[:, k + i:k + i + 1], ml.shape)
                al = al - c * q[0][i][:1, :]
                ar = ar - c * q[1][i][:1, :]
            m[e:, :128] = al
            m[e:, 128:] = ar

def chol_block(a, w, lfac, m, v, b, n=6):
    s, e = b * B, (b + 1) * B
    vb = v[...]
    w[s:e, s:e] = vb
    if b:
        part = dot(lfac[s:e, :s], w[:s, :s], NN)
        w[s:e, :s] = -dot(vb, part, NN)
    if b < n - 1:
        lfac[e:, s:e] = dot(a[e:, s:e], vb, NT)
        for j in range(b + 1, n):
            js, je = j * B, (j + 1) * B
            a[js:, js:je] = a[js:, js:je] - dot(lfac[js:, s:e], lfac[js:je, s:e], NT)

MESH = pl.DeviceIdType.MESH
NZ, NY, NX = 8, 4, 4
AXES = ("z", "y", "x", "c")
SIZES = {"z": NZ, "y": NY, "x": NX, "c": 2}
VM = pl.BlockSpec(memory_space=pltpu.VMEM)
ANY = pl.BlockSpec(memory_space=pl.ANY)
DMA = pltpu.SemaphoreType.DMA


def step_to(axis, hops):
    return lax.rem(lax.axis_index(axis) + hops, SIZES[axis])


def greet(peers):
    barrier = pltpu.get_barrier_semaphore()
    for axis, hops in peers:
        pl.semaphore_signal(barrier, inc=1, device_id={axis: step_to(axis, hops)}, device_id_type=MESH)
    pl.semaphore_wait(barrier, len(peers))


def send(src, dst, sems, k, axis, hops):
    copy = pltpu.make_async_remote_copy(
        src_ref=src, dst_ref=dst, send_sem=sems[0].at[k], recv_sem=sems[1].at[k],
        device_id={axis: step_to(axis, hops)}, device_id_type=MESH,
    )
    copy.start()
    return copy


RATE, HOP = 42e3, 2.0


def sketch_plan(d, cut, K):
    free, heap, plan, count, order = {}, [], [], 0, 0
    missing = {dz: NY * K for dz in range(NZ)}

    def post(when, what):
        nonlocal order
        order += 1
        heapq.heappush(heap, (when, order, what))

    def start(now, phase, way, step, dz, dy, lo, hi):
        nonlocal count
        axis = phase[1]
        end = max(now, free.get((axis, way), 0.0)) + d * (hi - lo) * 2 / RATE
        free[axis, way] = end
        job = (phase, axis, way, step, dz, dy, lo, hi, count)
        count += 1
        post(end + HOP, ("got", job))
        return job

    def both(now, phase, dz, dy, lo, hi):
        return [start(now, phase, way, 0, dz, dy, lo, hi) for way in (1, -1)]

    def share(now, axis, size, lag):
        end = max(now, free.get(axis, 0.0)) + size / (100e3 if axis == "c" else RATE / 2)
        free[axis] = end
        return end + lag

    first = both(0, "ly", 0, 0, 0, cut) + both(0, "rz", 0, 0, cut, K)
    first += both(0, "lz", 0, 0, 0, cut) + both(0, "ry", 0, 0, cut, K)
    plan.append(("got", None, first))
    missing[0] -= K
    now = 0.0
    rows = NY * d
    while heap:
        when, _, what = heapq.heappop(heap)
        now = max(now, when) + 0.05
        if what[0] == "got":
            job = what[1]
            phase, axis, way, step, dz, dy, lo, hi, _ = job
            dz, dy = (dz - way, dy) if axis == "z" else (dz, dy - way)
            mid = lo + ((hi - lo) // 128 + 1) // 2 * 128
            far = SIZES[axis] // 2
            new = []
            if step < far - 1:
                a, b = (lo, hi) if step < far - 2 else ((lo, mid) if way == 1 else (mid, hi))
                if b > a:
                    new.append(start(now, phase, way, step + 1, dz, dy, a, b))
            if phase in ("ly", "rz"):
                new += both(now, "lz" if phase == "ly" else "ry", dz, dy, lo, hi)
            plan.append(("got", job, new))
            missing[dz % NZ] -= hi - lo
            if not missing[dz % NZ]:
                post(now + 0.3, ("product", dz % NZ))
        elif what[0] == "product":
            plan.append(what)
            now += 1.5
            post(share(now, "c", rows * 512, 1.5), ("sum", what[1], 1))
        else:
            _, dz, stage = what
            plan.append(what)
            now += 0.2
            if stage == 1:
                post(share(now, "x", rows * 512, HOP + 1), ("sum", dz, 2))
            elif stage == 2:
                post(share(now, "c", rows * 512, 1.5), ("sum", dz, 3))
    return plan, count, now


def sketch_part(plan, t, slab, slab_copy, st, g, part, near, acc, far, gs, gr, ss, sr, own_sem):
    z, y, x, c = (lax.axis_index(axis) for axis in AXES)
    d = t.shape[0] * 8
    rows = NY * d
    half = st.shape[1] // 2

    def place(dz, dy, lo, hi):
        at = (lax.rem(z + dz + NZ, NZ) * NY + lax.rem(y + dy + NY, NY)) * d
        return g.at[pl.ds(at // 8, d // 8), :, lo:hi]

    def copy(job):
        phase, axis, way, step, dz, dy, lo, hi, k = job
        to = place(dz, dy, lo, hi)
        return pltpu.make_async_remote_copy(
            src_ref=t.at[:, :, lo:hi] if dz == dy == 0 else to, dst_ref=to, send_sem=gs.at[k], recv_sem=gr.at[k],
            device_id={axis: step_to(axis, 1 if way == 1 else SIZES[axis] - 1)}, device_id_type=MESH,
        )

    def rows_of(dz):
        return pl.multiple_of(lax.rem(z + dz, NZ) * rows, 8)

    def lanes_of(core):
        return pl.ds(pl.multiple_of(core * half, half), half)

    def remote(src, dst, k, axis, hops):
        return pltpu.make_async_remote_copy(
            src_ref=src, dst_ref=dst, send_sem=ss.at[k], recv_sem=sr.at[k],
            device_id={axis: step_to(axis, hops)}, device_id_type=MESH,
        )

    def exchange(dz, stage):
        k = dz * 5
        if stage == 1:
            return [remote(part.at[dz, :, lanes_of(1 - c)], near.at[dz], k, "c", 1)]
        if stage == 2:
            return [remote(acc.at[dz], far.at[dz, x], k + i, "x", i) for i in (1, 2, 3)]
        all_mine = st.at[pl.ds(rows_of(dz), rows), lanes_of(c)]
        return [remote(all_mine, all_mine, k + 4, "c", 1)]

    def begin(dz, stage):
        for one in exchange(dz, stage):
            one.start()

    keep = pltpu.make_async_copy(t, place(0, 0, 0, t.shape[2]), own_sem)
    kept = False
    for what in plan:
        if what[0] == "got":
            if what[1] is not None:
                copy(what[1]).wait_recv()
            for job in what[2]:
                copy(job).start()
            if what[1] is None:
                keep.start()
        elif what[0] == "product":
            dz = what[1]
            if not kept:
                keep.wait()
                slab_copy.wait()
                kept = True
            part[dz] = lax.dot_general(g[pl.ds(rows_of(dz) // 8, rows // 8)].reshape(rows, g.shape[2]), slab[...], (NT, ((), ())), preferred_element_type=F32)
            begin(dz, 1)
        else:
            _, dz, stage = what
            for one in exchange(dz, stage):
                one.wait_recv()
            if stage == 1:
                total = part[dz, :, lanes_of(c)] + near[dz]
                acc[dz] = total
                far[dz, x] = total
            elif stage == 2:
                total = far[dz, 0]
                for other in range(1, NX):
                    total = total + far[dz, other]
                st[pl.ds(rows_of(dz), rows), lanes_of(c)] = total
            if stage < 3:
                begin(dz, stage + 1)
    for what in plan:
        if what[0] == "got" and what[1] is not None:
            copy(what[1]).wait_send()
        elif what[0] == "sum":
            for one in exchange(what[1], what[2]):
                one.wait_send()


SLOTS = 3


def place(t):
    at_least = lambda k: (t + 32 - k) // 32
    i = at_least(1) + at_least(3) + at_least(6) + at_least(10) + at_least(15)
    j = t - i * (i + 1) // 2
    spare = at_least(21)
    return i, j * (1 - spare)


def gram_compute(s, gp):
    a = lax.axis_index("x") * 2 + lax.axis_index("c")
    for k in range(SLOTS):
        i, j = place(a * SLOTS + k)
        li = s[pl.ds(pl.multiple_of(i * B, B), B), :]
        lj = s[pl.ds(pl.multiple_of(j * B, B), B), :]
        gp[k * B:(k + 1) * B, :] = dot(li, lj, NT)


GRAM_PEERS = [("z", i) for i in range(1, NZ)] + [("y", i) for i in range(1, NY)] + [("x", i) for i in range(1, NX)] + [("c", 1)]
GRAM_COPIES = 7 + 3 + 7 + 3 + 1


def gram_exchange(gp, gz, own, gy, full, sems, base):
    x, c, z = lax.axis_index("x"), lax.axis_index("c"), lax.axis_index("z")
    q = gp.shape[0] // NZ
    copies = []
    ones = []
    for i in range(1, NZ):
        o = pl.multiple_of(step_to("z", i) * q, q)
        ones.append(send(gp.at[pl.ds(o, q)], gz.at[i - 1], sems, base + i - 1, "z", i))
    yield
    mine = pl.ds(pl.multiple_of(z * q, q), q)
    total = gp[mine, :]
    for i in range(1, NZ):
        ones[i - 1].wait_recv()
        total = total + gz[i - 1]
    own[...] = total
    twos = [send(own, gy.at[i - 1], sems, base + 6 + i, "y", i) for i in range(1, NY)]
    yield
    total = own[...]
    for i in range(1, NY):
        twos[i - 1].wait_recv()
        total = total + gy[i - 1]
    full[x, c, mine, :] = total
    here = full.at[x, c, mine]
    threes = [send(here, here, sems, base + 9 + i, "z", i) for i in range(1, NZ)]
    yield
    for t in threes:
        t.wait_recv()
    all_mine = full.at[x, c]
    fours = [send(all_mine, all_mine, sems, base + 16 + i, "x", i) for i in range(1, NX)]
    yield
    for t in fours:
        t.wait_recv()
    column = full.at[:, c]
    five = send(column, column, sems, base + 20, "c", 1)
    yield
    five.wait_recv()
    for t in (*ones, *twos, *threes, *fours, five):
        t.wait_send()


GRAM_SCRATCH = [pltpu.VMEM((SLOTS * B, B), F32), pltpu.VMEM((NZ - 1, SLOTS * B // NZ, B), F32), pltpu.VMEM((SLOTS * B // NZ, B), F32), pltpu.VMEM((NY - 1, SLOTS * B // NZ, B), F32)]


Z_ROWS = ((1, 0, 144), (1, 144, 136), (-1, 280, 144), (-1, 424, 136))
Y_ROWS = ((1, 0, 40), (1, 40, 32), (-1, 72, 40), (-1, 112, 32))
ZY_ROWS = ((1, 0, 72), (-1, 72, 72))
HALF = 384
WIDTH = 140
REST = WIDTH - 128
KINDS = (("z", "z", Z_ROWS), ("y", "y", Y_ROWS), ("zy", "y", ZY_ROWS), ("yz", "z", Y_ROWS))


def stream_specs():
    specs = []
    for kind, axis, rows in KINDS:
        for k, (way, o, n) in enumerate(rows):
            after = {"zy": tuple(("z", i) for i in range(4)), "yz": (("y", k),)}.get(kind, ())
            specs.append(((kind, k), axis, way, n * HALF * 4 * (NZ if kind == "y" else 1), after))
    return specs


def finish_plan():
    specs = {s[0]: s for s in stream_specs()}
    free, heap, plan, count, ended = {}, [], [], 0, set()

    def wire(now, axis, way, size):
        end = max(now, free.get((axis, way), 0.0)) + size / RATE
        free[axis, way] = end
        return end + HOP

    def post(when, what):
        nonlocal count
        count += 1
        heapq.heappush(heap, (when, count, what))

    def begin(now, name):
        _, axis, way, size, _ = specs[name]
        post(wire(now, axis, way, size), ("serve", name, 0))

    def gram_sends(now, stage):
        q = SLOTS * B * B * 4 // NZ
        if stage in (0, 2):
            when = max(wire(now, "z", way, 8 * q) for way in (1, -1)) + 1.5 * HOP
        elif stage == 1:
            when = max(wire(now, "y", way, 2 * q) for way in (1, -1)) + HOP
        else:
            when = now + (11.0 if stage == 3 else 3.5)
        post(when, ("gram", stage + 1))

    now = 1.5
    gram_sends(now, 0)
    now += 3.0
    zfirst = [n for n, s in specs.items() if not s[4] and s[1] == "z"]
    yfirst = [n for n, s in specs.items() if not s[4] and s[1] == "y"]
    early = zfirst[0:3:2]
    held = {1: yfirst, 2: [n for n in zfirst if n not in early]}

    def launch(names):
        for name in names:
            begin(now, name)
        plan.append(("begin", names))

    launch(early)
    plan.append(("tiles",))
    now += 3.4
    chol = []
    while heap or chol:
        if heap and (heap[0][0] <= now or not chol):
            when, _, what = heapq.heappop(heap)
            now = max(now, when)
            plan.append(what)
            if what[0] == "gram":
                now += 0.3
                if what[1] < 5:
                    gram_sends(now, what[1])
                    launch(held.get(what[1], []))
                else:
                    now += 1.0
                    chol = [c for b in range(6) for c in [("chol", b, p) for p in range(4)] + [("block", b)]]
            else:
                _, name, s = what
                _, axis, way, size, _ = specs[name]
                now += 0.1 + size / 3e6
                if s < SIZES[axis] - 2:
                    post(wire(now, axis, way, size), ("serve", name, s + 1))
                else:
                    ended.add(name)
                    for other, spec in specs.items():
                        if name in spec[4] and all(x in ended for x in spec[4]):
                            begin(now, other)
                            plan.append(("begin", [other]))
        else:
            what = chol.pop(0)
            plan.append(what)
            now += 1.35 if what[0] == "chol" else 2.0
            chol_end = now
    return plan, now, chol_end


class Stream:
    def __init__(self, axis, way, local, buf, sink, sems, base):
        self.axis, self.way, self.n = axis, way, SIZES[axis]
        self.local, self.buf, self.sink, self.sems, self.base = local, buf, sink, sems, base

    def block(self, back):
        n = self.n
        return lax.rem(lax.axis_index(self.axis) + (2 * n - back if self.way == 1 else back), n)

    def copy(self, s):
        return pltpu.make_async_remote_copy(
            src_ref=self.local(self.block(1)) if s == 0 else self.buf.at[s - 1],
            dst_ref=self.buf.at[s],
            send_sem=self.sems[0].at[self.base + s], recv_sem=self.sems[1].at[self.base + s],
            device_id={self.axis: step_to(self.axis, 1 if self.way == 1 else self.n - 1)}, device_id_type=MESH,
        )

    def serve(self, s):
        self.copy(s).wait_recv()
        total = self.buf[s] + self.local(self.block(2 + s))[...]
        if s < self.n - 2:
            self.buf[s] = total
            self.copy(s + 1).start()
        else:
            self.sink[...] = total

    def finish(self):
        for s in range(self.n - 1):
            self.copy(s).wait_send()


def sub_start(i):
    return pl.multiple_of(i * 140 // 8 * 8, 8)


RS_COPIES = 4 * 7 + 4 * 3 + 2 * 3 + 4 * 7


def whole_kernel(plan, t, slab_in, p, slab, slab_sem, st, g, part, near, acc, far, ts, tr, us, ur, own_sem, *rest):
    out, w, c, resz, resy = rest[:5]
    rest = rest[5:]
    zb, yb, zyb, yzb = rest[0:4], rest[4:8], rest[8:10], rest[10:14]
    hi, lo, gp, gz, own, gy, full, a, lfac, m, v, ss, rs, gs, gr = rest[14:]
    slab_copy = pltpu.make_async_copy(slab_in, slab, slab_sem)
    slab_copy.start()
    greet(GRAM_PEERS)
    sketch_part(plan, t, slab, slab_copy, st, g, part, near, acc, far, ts, tr, us, ur, own_sem)
    s = st
    sems = (ss, rs)
    tiles = slab.shape[1] // B
    exchange = gram_exchange(gp, gz, own, gy, full, (gs, gr), 0)
    gram_compute(s, gp)
    next(exchange)
    for k in range(s.shape[0] // B):
        turned = s[k * B:(k + 1) * B, :].T
        top = turned.astype(jnp.bfloat16)
        hi[:, k * B:(k + 1) * B] = top
        lo[:, k * B:(k + 1) * B] = (turned - top.astype(F32)).astype(jnp.bfloat16)

    def tile(t, _):
        part = slab[:, pl.ds(pl.multiple_of(t * B, B), B)]
        value = lax.dot_general(part, hi[...], (TN, ((), ())), preferred_element_type=F32)
        value = value + lax.dot_general(part, lo[...], (TN, ((), ())), preferred_element_type=F32)
        for k in range(8):
            q = t * 8 + k
            c[q // 35, pl.ds(pl.multiple_of(lax.rem(q, 35) * 16, 16), 16), :] = value[k * 16:(k + 1) * 16, :]
        return 0

    start = lax.rem(lax.axis_index("z") + NZ - 1, NZ) * (slab.shape[1] // NZ) // B
    def tiles_of(lo, hi):
        lax.fori_loop(lo, hi, lambda t, _: tile(lax.rem(start + t, tiles), 0), 0)

    streams, base = {}, 0
    for kind, axis, rows in KINDS:
        for k, (way, o, n) in enumerate(rows):
            buf, sink = {
                "z": lambda: (zb[k], resz.at[o:o + n]),
                "y": lambda: (yb[k], resy.at[:, o:o + n]),
                "zy": lambda: (zyb[k], out.at[o:o + n, 0:HALF]),
                "yz": lambda: (yzb[k], out.at[o:o + n, HALF:2 * HALF]),
            }[kind]()
            local = functools.partial(lambda i, kind, o, n: {
                "z": lambda: c.at[i, o:o + n, 0:HALF],
                "y": lambda: c.at[:, pl.ds(sub_start(i) + o, n), HALF:2 * HALF],
                "zy": lambda: resz.at[pl.ds(sub_start(i) + o, n)],
                "yz": lambda: resy.at[i, o:o + n],
            }[kind](), kind=kind, o=o, n=n)
            streams[kind, k] = Stream(axis, way, local, buf, sink, sems, base)
            base += SIZES[axis] - 1

    n = 6

    def act(what):
        if what[0] == "gram":
            next(exchange, None)
            if what[1] == 5:
                for i in range(n):
                    for j in range(i + 1):
                        t = i * (i + 1) // 2 + j
                        a[i * B:(i + 1) * B, j * B:(j + 1) * B] = full[t // 6, t // 3 % 2, (t % 3) * B:(t % 3 + 1) * B, :]
        elif what[0] == "begin":
            for name in what[1]:
                streams[name].copy(0).start()
        elif what[0] == "serve":
            streams[what[1]].serve(what[2])
        elif what[0] == "tiles":
            tiles_of(14, tiles)

    plan = finish_plan()[0]
    first = next(i for i, what in enumerate(plan) if what[0] == "chol")
    last = max(i for i, what in enumerate(plan) if what[0] == "block")
    table, key = {}, None
    for what in plan[first:last + 1]:
        if what[0] == "chol":
            key = what[1], what[2]
        elif what[0] == "block":
            key = what[1], 4
        else:
            table.setdefault(key, []).append(what)

    tiles_of(0, 3)
    streams["z", 0].copy(0).start()
    tiles_of(10, 14)
    streams["z", 2].copy(0).start()
    tiles_of(3, 10)
    w[...] = jnp.zeros_like(w)
    p[:, 24:, :] = jnp.zeros((p.shape[0], 8, 128), F32)
    for what in plan[1:first]:
        act(what)
    row_of = lax.broadcasted_iota(jnp.int32, (B, B), 0)
    col_of = lax.broadcasted_iota(jnp.int32, (B, B), 1)
    eye = jnp.where(row_of == col_of, 1.0, 0.0).astype(F32)

    def step(b, _):
        o = pl.multiple_of(b * B, B)
        m[:, :B] = a[pl.ds(o, B), pl.ds(o, B)]
        m[:, B:] = eye
        for piece in range(5):
            if piece < 4:
                factor_panels(m, v, 4 * piece, 4 * piece + 4)
            for k in range(n):
                if piece == 4 or table.get((k, piece)):
                    @pl.when(b == k)
                    def _():
                        if piece == 4:
                            chol_block(a, w, lfac, m, v, k)
                        for what in table.get((k, piece), ()):
                            act(what)
        return 0

    lax.fori_loop(0, n, step, 0)
    odd = lax.rem(lax.axis_index("y"), 2)
    skip = out.shape[0] - WIDTH

    def share(lo, hi):
        return jnp.where(odd == 1, out[skip:, lo:hi], out[:WIDTH, lo:hi])

    def put(b, value):
        for q in range(B // 8):
            to, i = divmod(b * (B // 8) + q, 3)
            p[to, 8 * i:8 * i + 8, :] = value[8 * q:8 * q + 8, :128]
            p[to, 24:, REST * i:REST * i + REST] = value[8 * q:8 * q + 8, 128:]

    rest_of_plan = plan[last + 1:]
    ready = 1 + max([i for i, what in enumerate(rest_of_plan) if what[0] == "serve" and what[1][0] == "zy"], default=-1)
    for what in rest_of_plan[:ready]:
        act(what)
    half = share(0, HALF)
    begun = {}
    for b in range(n):
        e = min((b + 1) * B, HALF)
        begun[b] = dot(w[b * B:(b + 1) * B, :e], half[:, :e], NT)
        if b < HALF // B:
            put(b, begun[b])
        else:
            a[b * B:(b + 1) * B, :WIDTH] = begun[b]
    for what in rest_of_plan[ready:]:
        act(what)
    half = share(HALF, 2 * HALF)
    for b in range(HALF // B, n):
        e = (b + 1) * B - HALF
        put(b, a[b * B:(b + 1) * B, :WIDTH] + dot(w[b * B:(b + 1) * B, HALF:HALF + e], half[:, :e], NT))
    for stream in streams.values():
        stream.finish()


def whole(t, slab):
    d, K = t.shape
    R = slab.shape[0]
    plan, count, _ = sketch_plan(d, K // 128 * 2 // 5 * 128, K)
    C, rows = NZ * NY * d, NY * d
    bf = jnp.bfloat16
    vm = lambda *shape: pltpu.VMEM(shape, F32)
    HBM = pl.BlockSpec(memory_space=pltpu.HBM)
    return pl.pallas_call(
        functools.partial(whole_kernel, plan),
        out_shape=jax.ShapeDtypeStruct((NZ * NY, d + 8, 128), F32),
        in_specs=[HBM, HBM], out_specs=VM,
        scratch_shapes=[
            pltpu.VMEM((R, K), bf), DMA, vm(C, R), pltpu.VMEM((C // 8, 8, K), bf),
            vm(NZ, rows, R), vm(NZ, rows, R // 2), vm(NZ, rows, R // 2), vm(NZ, NX, rows, R // 2),
            DMA((count,)), DMA((count,)), DMA((40,)), DMA((40,)), DMA,
            vm(144, C), vm(C, C),
            vm(NZ, 560, C), vm(560, HALF), vm(NZ, 144, HALF),
            *[vm(NZ - 1, n, HALF) for _, _, n in Z_ROWS],
            *[vm(NY - 1, NZ, n, HALF) for _, _, n in Y_ROWS],
            *[vm(NY - 1, n, HALF) for _, _, n in ZY_ROWS],
            *[vm(NZ - 1, n, HALF) for _, _, n in Y_ROWS],
            pltpu.VMEM((R, C), bf), pltpu.VMEM((R, C), bf),
            *GRAM_SCRATCH, vm(NX, 2, SLOTS * B, B), vm(C, C), vm(C, C), vm(B, 2 * B), vm(B, B),
            DMA((RS_COPIES,)), DMA((RS_COPIES,)), DMA((GRAM_COPIES,)), DMA((GRAM_COPIES,)),
        ],
        compiler_params=pltpu.CompilerParams(collective_id=0, has_side_effects=True, vmem_limit_bytes=63 * 2**20), name="whole",
    )(t.reshape(d // 8, 8, K), slab)


def unpack_kernel(q, out):
    for k in range(q.shape[0]):
        out[:, WIDTH * k:WIDTH * k + 128] = q[k, :24, :]
        for i in range(3):
            out[8 * i:8 * i + 8, WIDTH * k + 128:WIDTH * (k + 1)] = q[k, 24:, REST * i:REST * i + REST]


def body(slab, test):
    p = whole(test.T, slab)
    q = lax.all_to_all(p, ("z", "y"), 0, 0, tiled=True)
    return pl.pallas_call(
        unpack_kernel, out_shape=jax.ShapeDtypeStruct((24, slab.shape[1]), F32),
        in_specs=[VM], out_specs=VM, name="unpack",
    )(q)


def solution(mesh):
    split = Mesh(mesh.devices.reshape(NZ, NY, NX, 2), AXES)
    return jax.shard_map(
        body, mesh=split, in_specs=(P(("z", "y"), ("x", "c")), P(("x", "c"), ("z", "y"))),
        out_specs=P(("z", "y"), ("x", "c")), check_vma=False,
    )
```
